1024 devices in a mesh: section: 8 (over x, core), expert: 32 (over y, z_lo), replica: 4 (over z_hi).
Axes of the slice: x: 4, y: 4, z: 32 (z_hi: 4, z_lo: 8; z = z_hi * 8 + z_lo), core: 2. Of those that a mesh axis runs over, the one named last changes fastest.
Arguments:
- token_grads: bfloat16 [8, 2048, 3584], P('section', 'expert', 'replica'), may hold values from -6 to 6
- routing: int32 [8, 2048, 4], P('section', 'expert'), may hold values from 0 to 7, all different within a row; in each aligned block of 64 rows (0 to 63, 64 to 127, ..., all dimensions but the last counted through in order) at most 34 rows name the same one
- gate_weights: float32 [8, 2048, 4], P('section', 'expert'), may hold values from 0.1 to 1
- layer_inputs: bfloat16 [8, 2048, 3584], P('section', 'expert', 'replica'), may hold values from -6 to 6
- w_gate: bfloat16 [8, 3584, 8192], P('section', 'replica', 'expert'), may hold values from -0.09375 to 0.09375
- w_up: bfloat16 [8, 3584, 8192], P('section', 'replica', 'expert'), may hold values from -0.09375 to 0.09375
- w_down: bfloat16 [8, 3584, 8192], P('section', 'replica', 'expert'), may hold values from -0.09375 to 0.09375
Outputs:
- upstream: bfloat16 [8, 2048, 3584], P('section', 'expert', 'replica')
- grad_gate: bfloat16 [8, 3584, 8192], P('section', 'replica', 'expert')
- grad_up: bfloat16 [8, 3584, 8192], P('section', 'replica', 'expert')
- grad_down: bfloat16 [8, 3584, 8192], P('section', 'replica', 'expert')
The draws below stay inside these ranges and needn't reach their ends.
Inputs may be any that keep to these rules, and one draw needn't show every extreme that they name: `routing`: each token names 4 different experts. Among the 64 tokens of one group no expert is named more than 34 times, and in every draw some group names some expert exactly 34 times.
All inputs are finite; a program needn't handle non-finite values.
Results may differ from the reference program's by a relative error of at most 0.0064.
Values may be sent and summed in bfloat16 or wider, within the bound.
A program may use at most 32 MiB of HBM per device.

```python
import math
import jax
import jax.numpy as jnp
import numpy as np
from jax import lax

D = 3584
FFW = 1024
SHARES = 4
EXPERTS = 8
TOP = 4
TOK_DEV = 64
CAP = 34
TOKENS = 2048
N_SECTION = 8
N_EXPERT = 32


def shard_levels(own_key, dims, pieces, least, largest):
    loudness = 1.0
    for axis_at, parts in pieces:
        heights = jax.random.uniform(jax.random.fold_in(jax.random.fold_in(own_key, 6), axis_at), (parts,), jnp.float32, least / len(pieces), largest / len(pieces))
        loudness = loudness * jnp.repeat(jnp.exp(heights), dims[axis_at] // parts).reshape((-1,) + (1,) * (len(dims) - 1 - axis_at))
    return loudness


def routed_block(rng, own, number, rows, count, top, most, slope):
    ranking = jax.random.permutation(rng, count)
    heavy_load, ordinary = shares(count, rows * top, most, slope, True), shares(count, rows * top, most, slope, False)
    places = jnp.arange(count)

    def named(lengths, turn):
        used = int((lengths > 0).sum())
        fixed = max(1, used // 4)
        moved = fixed + (places - fixed + turn * (used - fixed)) % max(1, count - fixed)
        return jnp.zeros((count,), jnp.int32).at[ranking[jnp.where(places < fixed, places, moved)]].set(jnp.asarray(lengths, jnp.int32))

    lengths = jnp.where(number % 4 == 0, named(heavy_load, number // 4), named(ordinary, number - number // 4 - 1))
    mixed = jax.random.permutation(jax.random.fold_in(own, 3), count)
    donor, taker = mixed[0:count // 2 * 2:2], mixed[1:count // 2 * 2:2]
    room = jnp.minimum(lengths[donor] - 1, most - lengths[taker]) // 2
    room = jnp.where((donor == ranking[0]) | (taker == ranking[0]) | (lengths[taker] == 0), 0, jnp.maximum(room, 0))
    moved = jax.random.randint(jax.random.fold_in(own, 4), (count // 2,), 0, 1 << 20) % (room + 1)
    lengths = lengths.at[donor].add(-moved).at[taker].add(moved)
    items = jnp.searchsorted(jnp.cumsum(lengths), jnp.arange(rows * top), side="right").astype(jnp.int32)
    grid = items.reshape(top, rows).T
    grid = grid[jax.random.permutation(jax.random.fold_in(own, 1), rows)]
    turn = jax.random.randint(jax.random.fold_in(own, 2), (rows, 1), 0, top)
    return jnp.take_along_axis(grid, (jnp.arange(top)[None, :] + turn) % top, axis=1)


def shares(number_of, total, reach, skew, full):
    weights = [(1 << 20) // math.isqrt(standing ** skew) + 1 for standing in range(1, number_of + 1)]
    largest = reach if full else min(reach, max(-(-total // number_of), total * weights[0] // sum(weights)))
    least = 1 if total - largest >= number_of - 1 else 0
    holding, rest = [largest] + [least] * (number_of - 1), total - largest - least * (number_of - 1)
    while rest > 0:
        free = [i for i in range(1, number_of) if holding[i] < largest] or [i for i in range(1, number_of) if holding[i] < reach]
        whole, left = sum([weights[i] for i in free]), rest
        for i in free:
            more = min(reach - holding[i], max(1, left * weights[i] // whole), rest)
            holding[i] = holding[i] + more
            rest = rest - more
    return np.array(holding)


def normal_values(own_key, dims, deviation, limit, split=(), kind=jnp.bfloat16):
    drawn = jax.random.normal(own_key, dims, jnp.float32) * deviation
    if len(split) > 0:
        drawn = shard_levels(own_key, dims, split, -0.22, 0.18) * drawn
    return jnp.clip(drawn, min=-limit, max=limit).astype(kind)


def setup_inputs(seed: int = 0) -> dict:
    streams_of = jax.random.split(jax.random.key(seed), 8)
    token_grads = normal_values(streams_of[0], (N_SECTION, TOKENS, D), 1.0, 6.0, ((0, 8), (1, 32), (2, 4)))
    routing_keys = jax.random.split(jax.random.fold_in(streams_of[1], 1), N_SECTION * TOKENS // TOK_DEV)
    routing_turns = jax.random.permutation(jax.random.fold_in(streams_of[1], 3), N_SECTION * TOKENS // TOK_DEV)
    routing = jax.vmap(lambda own, number: routed_block(jax.random.fold_in(streams_of[1], 2), own, number, TOK_DEV, EXPERTS, TOP, CAP, 2))(routing_keys, routing_turns).reshape((N_SECTION, TOKENS, TOP))
    gate_weights = jnp.clip(jnp.exp(math.log(1.0) - 2.3025851 * jax.random.uniform(streams_of[2], (N_SECTION, TOKENS, TOP), jnp.float32) ** shard_levels(streams_of[2], (N_SECTION, TOKENS, TOP), ((0, 8), (1, 32)), -0.2, 0.2)), 0.1, 1.0)
    layer_inputs = normal_values(streams_of[3], (N_SECTION, TOKENS, D), 1.0, 6.0, ((0, 8), (1, 32), (2, 4)))
    w_gate = normal_values(streams_of[4], (N_SECTION, D, EXPERTS * FFW), D ** -0.5, 0.09375, ((0, 8), (1, 4), (2, 32)))
    w_up = normal_values(streams_of[5], (N_SECTION, D, EXPERTS * FFW), D ** -0.5, 0.09375, ((0, 8), (1, 4), (2, 32)))
    w_down = normal_values(streams_of[6], (N_SECTION, D, EXPERTS * FFW), D ** -0.5, 0.09375, ((0, 8), (1, 4), (2, 32)))
    return {"token_grads": token_grads, "routing": routing, "gate_weights": gate_weights, "layer_inputs": layer_inputs, "w_gate": w_gate, "w_up": w_up, "w_down": w_down}


def slot_index(routes, n_experts, capacity):
    flat_route = routes.reshape(-1).astype(jnp.int32)
    one_hot = (flat_route[:, None] == jnp.arange(n_experts, dtype=jnp.int32)[None, :]).astype(jnp.int32)
    before = jnp.cumsum(one_hot, axis=0) - one_hot
    rank_in = jnp.sum(before * one_hot, axis=1)
    return (flat_route * capacity + rank_in).astype(jnp.int32)


def dispatch_rows(grad_rows, routes, weights, n_experts, capacity):
    feature_width = grad_rows.shape[1]
    scaled = (grad_rows.astype(jnp.float32)[:, None, :] * weights.astype(jnp.float32)[:, :, None]).reshape(-1, feature_width)
    positions = slot_index(routes, n_experts, capacity)
    blank_rows = jnp.zeros((n_experts * capacity, feature_width), jnp.float32)
    return blank_rows.at[positions].set(scaled).astype(jnp.bfloat16)


def place_rows(inputs, routes, n_experts, capacity):
    feature_width = inputs.shape[1]
    chosen = routes.shape[1]
    copies = jnp.broadcast_to(inputs[:, None, :], (inputs.shape[0], chosen, feature_width)).reshape(-1, feature_width)
    positions = slot_index(routes, n_experts, capacity)
    blank_rows = jnp.zeros((n_experts * capacity, feature_width), inputs.dtype)
    return blank_rows.at[positions].set(copies)


def activations(gate_pre, up_pre, grad_hidden):
    sigmoid_gate = jax.nn.sigmoid(gate_pre)
    activated = gate_pre * sigmoid_gate
    hidden = (activated * up_pre).astype(jnp.bfloat16)
    slope_term = sigmoid_gate * (1.0 + gate_pre * (1.0 - sigmoid_gate))
    d_gate = (grad_hidden * up_pre * slope_term).astype(jnp.bfloat16)
    d_up = (grad_hidden * activated).astype(jnp.bfloat16)
    return hidden, d_gate, d_up


def expert_backward(received, saved, gate_mat, up_mat, down_mat):
    gate_pre = jnp.dot(saved, gate_mat, preferred_element_type=jnp.float32)
    up_pre = jnp.dot(saved, up_mat, preferred_element_type=jnp.float32)
    grad_hidden = jnp.dot(received, down_mat, preferred_element_type=jnp.float32)
    hidden, d_gate, d_up = activations(gate_pre, up_pre, grad_hidden)
    block_width = FFW // SHARES
    back_parts = []
    for share_id in range(SHARES):
        start_col = share_id * block_width
        stop_col = start_col + block_width
        part_sum = (jnp.dot(d_gate[:, start_col:stop_col], gate_mat[:, start_col:stop_col].T, preferred_element_type=jnp.float32)
                    + jnp.dot(d_up[:, start_col:stop_col], up_mat[:, start_col:stop_col].T, preferred_element_type=jnp.float32))
        back_parts.append(part_sum.astype(jnp.bfloat16))
    back_rows = jnp.stack(back_parts, axis=0)
    grad_g = jnp.dot(saved.T, d_gate, preferred_element_type=jnp.float32).astype(jnp.bfloat16)
    grad_u = jnp.dot(saved.T, d_up, preferred_element_type=jnp.float32).astype(jnp.bfloat16)
    grad_d = jnp.dot(received.T, hidden, preferred_element_type=jnp.float32).astype(jnp.bfloat16)
    return back_rows, grad_g, grad_u, grad_d


def reference(token_grads, routing, gate_weights, layer_inputs, w_gate, w_up, w_down):
    n_experts = EXPERTS
    capacity = CAP
    upstream_list = []
    gate_list = []
    up_list = []
    down_list = []
    for section_id in range(N_SECTION):
        grad_rows = token_grads[section_id].reshape(N_EXPERT, TOK_DEV, D)
        inputs = layer_inputs[section_id].reshape(N_EXPERT, TOK_DEV, D)
        routes = routing[section_id].reshape(N_EXPERT, TOK_DEV, TOP)
        weights = gate_weights[section_id].reshape(N_EXPERT, TOK_DEV, TOP)

        def send_one(items):
            return (dispatch_rows(items[0], items[1], items[2], n_experts, capacity),
                    place_rows(items[3], items[1], n_experts, capacity))

        outgoing, placed = lax.map(send_one, (grad_rows, routes, weights, inputs))
        arrived = jnp.transpose(outgoing.reshape(N_EXPERT, n_experts, capacity, D), (1, 0, 2, 3)).reshape(n_experts, N_EXPERT * capacity, D)
        saved_all = jnp.transpose(placed.reshape(N_EXPERT, n_experts, capacity, D), (1, 0, 2, 3)).reshape(n_experts, N_EXPERT * capacity, D)

        def per_expert(matrix):
            return jnp.transpose(matrix.reshape(D, n_experts, FFW), (1, 0, 2))

        def expert_one(items):
            return expert_backward(items[0], items[1], items[2], items[3], items[4])

        back_rows, grad_g, grad_u, grad_d = lax.map(
            expert_one, (arrived, saved_all, per_expert(w_gate[section_id]), per_expert(w_up[section_id]), per_expert(w_down[section_id])))
        merged = jnp.sum(back_rows.astype(jnp.float32), axis=1)
        returned = jnp.transpose(merged.reshape(n_experts, N_EXPERT, capacity, D), (1, 0, 2, 3)).reshape(N_EXPERT, n_experts * capacity, D)

        def combine_one(items):
            table, group_routes = items
            positions = slot_index(group_routes, n_experts, capacity)
            picked = table[positions].reshape(TOK_DEV, TOP, D)
            return jnp.sum(picked, axis=1).astype(jnp.bfloat16)

        input_grad = lax.map(combine_one, (returned, routes)).reshape(TOKENS, D)

        def joined(grad_blocks):
            return jnp.transpose(grad_blocks, (1, 0, 2)).reshape(D, n_experts * FFW)

        upstream_list.append(input_grad)
        gate_list.append(joined(grad_g))
        up_list.append(joined(grad_u))
        down_list.append(joined(grad_d))
    shifted = upstream_list[1:] + [jnp.zeros((TOKENS, D), jnp.bfloat16)]
    return (jnp.stack(shifted, axis=0), jnp.stack(gate_list, axis=0),
            jnp.stack(up_list, axis=0), jnp.stack(down_list, axis=0))
```

```python
import jax
import jax.numpy as jnp
from jax import lax
from jax.experimental import pallas as pl
from jax.experimental.pallas import tpu as pltpu
from jax.sharding import PartitionSpec as P

MESH = pl.DeviceIdType.MESH
SHARES = 4
NY, NZ, NR = 4, 8, 4
EXPERTS = 8
TOK = 64
CAP = 34
D = 896
H = 256
ROWS = NZ * CAP
TOKS = NZ * TOK
HALF = TOK // 2
PARTS = ((0, 96), (96, 96), (192, 80))
VMEM_LIMIT = 60 * 1024 * 1024


def remote(src, dst, send_sem, recv_sem, **where):
    return pltpu.make_async_remote_copy(
        src_ref=src, dst_ref=dst, send_sem=send_sem, recv_sem=recv_sem,
        device_id=where, device_id_type=MESH,
    )


def rows_of(ref, start, size):
    return ref.at[pl.ds(pl.multiple_of(start, 16), size), :]


def grid_place():
    me = lax.axis_index("expert")
    y, z = me // NZ, me % NZ
    return me, y, z, (y + 1) % NY * NZ + z, (y + NY - 1) % NY * NZ + z


def greet(me, z, up, down):
    barrier = pltpu.get_barrier_semaphore()
    for peer in (up, down):
        pl.semaphore_signal(barrier, inc=1, device_id={"expert": peer}, device_id_type=MESH)

    @pl.when(z > 0)
    def _():
        pl.semaphore_signal(barrier, inc=1, device_id={"expert": me - 1}, device_id_type=MESH)

    @pl.when(z < NZ - 1)
    def _():
        pl.semaphore_signal(barrier, inc=1, device_id={"expert": me + 1}, device_id_type=MESH)

    pl.semaphore_wait(barrier, 4 - (NZ - z) // NZ - (z + 1) // NZ)


def gather_kernel(b_ref, m_ref, ball, mall, own_sem,
                  zb_send, zb_recv, zm_send, zm_recv,
                  yb_send, yb_recv, ym_send, ym_recv,
                  fb_send, fb_recv, fm_send, fm_recv):
    me, y, z, up, down = grid_place()
    greet(me, z, up, down)
    own_b = pltpu.make_async_copy(b_ref, rows_of(ball, me * TOK, TOK), own_sem.at[0])
    own_m = pltpu.make_async_copy(m_ref, mall.at[me], own_sem.at[1])
    own_b.start()
    own_m.start()
    own_b.wait()
    own_m.wait()
    sides = ((me + 1, z < NZ - 1), (me - 1, z > 0))
    peers = (up, down)

    def z_copies(side, t, zz):
        block = y * NZ + zz
        to = sides[side][0]
        b = rows_of(ball, block * TOK, TOK)
        return (
            remote(b, b, zb_send.at[side, t], zb_recv.at[side, t], expert=to),
            remote(mall.at[block], mall.at[block], zm_send.at[side, t], zm_recv.at[side, t], expert=to),
        )

    def y_copies(way, col, zz):
        block = col * NZ + zz
        b = rows_of(ball, block * TOK, TOK)
        return (
            remote(b, b, yb_send.at[way, zz], yb_recv.at[way, zz], expert=peers[way]),
            remote(mall.at[block], mall.at[block], ym_send.at[way, zz], ym_recv.at[way, zz], expert=peers[way]),
        )

    def far_copy(way, col, zz):
        b = rows_of(ball, (col * NZ + zz) * TOK + way * HALF, HALF)
        return remote(b, b, fb_send.at[way, zz], fb_recv.at[way, zz], expert=peers[way])

    def far_meta(col, zz):
        block = col * NZ + zz
        return remote(mall.at[block], mall.at[block], fm_send.at[zz], fm_recv.at[zz], expert=up)

    came_up, came_down, far = (y + NY - 1) % NY, (y + 1) % NY, (y + 2) % NY

    def step(t, carry):
        for side in (0, 1):
            zz = z + t if side else z - t
            inside = (zz >= 0) & (zz < NZ)

            @pl.when(inside & (t > 0))
            def _():
                for c in z_copies(side, t - 1, zz):
                    c.wait_recv()

            @pl.when(inside & sides[side][1])
            def _():
                for c in z_copies(side, t, zz):
                    c.start()

            @pl.when(inside & ((t > 0) if side else (t >= 0)))
            def _():
                for way in (0, 1):
                    for c in y_copies(way, y, zz):
                        c.start()

        for side in (0, 1):
            zz = z + (t - 1) if side else z - (t - 1)
            inside = (zz >= 0) & (zz < NZ) & ((t > 1) if side else (t > 0))

            @pl.when(inside)
            def _():
                for c in y_copies(0, came_up, zz):
                    c.wait_recv()
                far_copy(0, came_up, zz).start()
                far_meta(came_up, zz).start()
                for c in y_copies(1, came_down, zz):
                    c.wait_recv()
                far_copy(1, came_down, zz).start()

        return carry

    lax.fori_loop(0, NZ + 1, step, 0)

    def finish(zz, carry):
        for way in (0, 1):
            far_copy(way, far, zz).wait_recv()
            far_copy(way, (came_up, came_down)[way], zz).wait_send()
            for c in y_copies(way, y, zz):
                c.wait_send()
        far_meta(far, zz).wait_recv()
        far_meta(came_up, zz).wait_send()
        for side in (0, 1):
            src = z + zz if side else z - zz

            @pl.when((src >= 0) & (src < NZ) & sides[side][1])
            def _():
                for c in z_copies(side, zz, src):
                    c.wait_send()

        return carry

    lax.fori_loop(0, NZ, finish, 0)


def all_tokens(block, meta):
    dma = pltpu.SemaphoreType.DMA
    return pl.pallas_call(
        gather_kernel,
        out_shape=(
            jax.ShapeDtypeStruct((NY * TOKS, 2 * D), jnp.bfloat16),
            jax.ShapeDtypeStruct((NY * NZ, 16, 128), jnp.float32),
        ),
        in_specs=[pl.BlockSpec(memory_space=pltpu.VMEM)] * 2,
        out_specs=(pl.BlockSpec(memory_space=pltpu.VMEM),) * 2,
        scratch_shapes=[dma((2,))] + [dma((2, NZ))] * 10 + [dma((NZ,))] * 2,
        compiler_params=pltpu.CompilerParams(
            collective_id=0, has_side_effects=True, vmem_limit_bytes=24 * 1024 * 1024
        ),
    )(block, meta)


def over_rows(left, right):
    return lax.dot_general(
        left, right, (((0,), (0,)), ((), ())), preferred_element_type=jnp.float32
    )


def over_cols(left, right):
    return lax.dot_general(
        left, right, (((1,), (1,)), ((), ())), preferred_element_type=jnp.float32
    )


def expert_kernel(ball, mall, wg, wu, wd, t_ref, gg, gu, gd,
                  pick, xs, gs, part, snd, rcv, act, wcat, back, gacc,
                  rs_send, rs_recv, ag_send, ag_recv):
    r = lax.axis_index("replica")
    e = lax.axis_index("expert") // SHARES
    nxt, prv = (r + 1) % NR, (r + NR - 1) % NR
    peers = (nxt, prv)
    barrier = pltpu.get_barrier_semaphore()
    for peer in peers:
        pl.semaphore_signal(barrier, inc=1, device_id={"replica": peer}, device_id_type=MESH)

    for d in (0, 1):
        wcat[d, :, 0:128] = wg[:, 128 * d:128 * d + 128]
        wcat[d, :, 128:256] = wu[:, 128 * d:128 * d + 128]

    lane = lax.broadcasted_iota(jnp.int32, (1, 128), 1)
    first = lane < TOK
    row = lax.broadcasted_iota(jnp.int32, (ROWS, 128), 0).astype(jnp.float32)
    which = lax.broadcasted_iota(jnp.int32, (NZ, EXPERTS, 128), 1)

    pl.semaphore_wait(barrier, 2)

    def rs_copy(d, s, k):
        at, size = PARTS[k]
        return remote(snd.at[d, s, at:at + size, :], rcv.at[d, s, at:at + size, :],
                      rs_send.at[d, s, k], rs_recv.at[d, s, k], replica=peers[d])

    def stage(d, s, k, c):
        at, size = PARTS[k]
        rows = pl.ds(pl.multiple_of(c * ROWS + at, 16), size)
        for kind in range(3):
            mine = part[rows, 256 * kind + 128 * d:256 * kind + 128 * d + 128]
            if s:
                mine = mine + rcv[d, s - 1, at:at + size, 128 * kind:128 * kind + 128].astype(jnp.float32)
            snd[d, s, at:at + size, 128 * kind:128 * kind + 128] = mine.astype(jnp.bfloat16)
        rs_copy(d, s, k).start()

    def chunk(q, carry):
        c = (r + 3 - 2 * q + 3 * (q // 2)) % NR
        rows = pl.ds(pl.multiple_of(c * ROWS, 16), ROWS)
        toks = pl.ds(pl.multiple_of(c * TOKS, 16), TOKS)
        meta = mall[pl.ds(c * NZ, NZ)]
        slots = jnp.sum(jnp.where(which == e, meta[:, 0:8, :], 0.0), axis=1)
        scale = jnp.sum(jnp.where(which == e, meta[:, 8:16, :], 0.0), axis=1)
        total = jnp.zeros((ROWS, 128), jnp.float32)
        for p in range(NZ // 2):
            slot = jnp.where(first, slots[2 * p:2 * p + 1], slots[2 * p + 1:2 * p + 2])
            w = jnp.where(first, scale[2 * p:2 * p + 1], scale[2 * p + 1:2 * p + 2])
            base = jnp.where(first, float(CAP * 2 * p), float(CAP * (2 * p + 1)))
            goal = jnp.where(slot >= 0.0, slot + base, -1.0)
            hit = row == goal
            total = total + jnp.where(hit, w, 0.0)
            pick[rows, 128 * p:128 * p + 128] = jnp.where(hit, 1.0, 0.0).astype(jnp.bfloat16)
        weight = jnp.sum(total, axis=1, keepdims=True)
        sel = pick[rows, :]
        x = jnp.dot(sel, ball[toks, 0:D], preferred_element_type=jnp.float32).astype(jnp.bfloat16)
        xs[rows, :] = x
        g = jnp.dot(sel, ball[toks, D:2 * D], preferred_element_type=jnp.float32)
        g = (g * weight).astype(jnp.bfloat16)
        gs[rows, :] = g
        part[rows, 0:256] = jnp.dot(x, wg[...], preferred_element_type=jnp.float32)
        part[rows, 256:512] = jnp.dot(x, wu[...], preferred_element_type=jnp.float32)
        part[rows, 512:768] = jnp.dot(g, wd[...], preferred_element_type=jnp.float32)
        for d in (0, 1):
            @pl.when(q == d)
            def _():
                for k in range(len(PARTS)):
                    stage(d, 0, k, c)

        return carry

    lax.fori_loop(0, NR, chunk, 0)

    for s in (1, 2):
        for k in range(len(PARTS)):
            for d in (0, 1):
                rs_copy(d, s - 1, k).wait_recv()
                stage(d, s, k, (r + NR - 1 - s) % NR if d == 0 else (r + 1 + s) % NR)

    def ag_copy(d, s, k, c):
        at, size = PARTS[k]
        there = act.at[d, pl.ds(pl.multiple_of(c * ROWS + at, 16), size), :]
        return remote(there, there, ag_send.at[d, s, k], ag_recv.at[d, s, k], replica=peers[d])

    for k, (at, size) in enumerate(PARTS):
        for d in (0, 1):
            rs_copy(d, 2, k).wait_recv()
            rows = pl.ds(pl.multiple_of(r * ROWS + at, 16), size)
            full = [
                part[rows, 256 * kind + 128 * d:256 * kind + 128 * d + 128]
                + rcv[d, 2, at:at + size, 128 * kind:128 * kind + 128].astype(jnp.float32)
                for kind in range(3)
            ]
            gate, up, dh = full
            sg = jax.nn.sigmoid(gate)
            a = gate * sg
            act[d, rows, 0:128] = (a * up).astype(jnp.bfloat16)
            act[d, rows, 128:256] = (dh * up * (sg * (1.0 + gate * (1.0 - sg)))).astype(jnp.bfloat16)
            act[d, rows, 256:384] = (dh * a).astype(jnp.bfloat16)
            ag_copy(d, 0, k, r).start()

    def spread(c):
        rows = pl.ds(pl.multiple_of(c * ROWS, 16), ROWS)
        toks = pl.ds(pl.multiple_of(c * TOKS, 16), TOKS)
        t_ref[toks, :] = over_rows(pick[rows, :], back[rows, :].astype(jnp.bfloat16)).astype(jnp.bfloat16)

    def arrive(k, carry):
        for d in (0, 1):
            c = (r + NR - k) % NR if d == 0 else (r + k) % NR

            @pl.when(k > 0)
            def _():
                for piece in range(len(PARTS)):
                    ag_copy(d, k - 1, piece, c).wait_recv()

                    @pl.when(k < NR - 1)
                    def _():
                        ag_copy(d, k, piece, c).start()

        for d in (0, 1):
            c = (r + NR - k) % NR if d == 0 else (r + k) % NR
            rows = pl.ds(pl.multiple_of(c * ROWS, 16), ROWS)
            both = act[d, rows, 128:384]
            more = over_cols(both, wcat[d])
            fresh = k < 3 if d == 0 else k == 1

            @pl.when(fresh)
            def _():
                back[rows, :] = more

            @pl.when(jnp.logical_not(fresh))
            def _():
                back[rows, :] = back[rows, :] + more

            up_down = over_rows(xs[rows, :], both)
            hid = over_rows(gs[rows, :], act[d, rows, 0:128])

            @pl.when(k == 0)
            def _():
                gacc[d, :, 128:384] = up_down
                gacc[d, :, 0:128] = hid

            @pl.when(k > 0)
            def _():
                gacc[d, :, 128:384] = gacc[d, :, 128:384] + up_down
                gacc[d, :, 0:128] = gacc[d, :, 0:128] + hid

        @pl.when(k % 2 == 0)
        def _():
            spread((r + k) % NR)

        @pl.when(k == 3)
        def _():
            spread((r + 1) % NR)
            spread((r + 3) % NR)

        return carry

    lax.fori_loop(0, NR, arrive, 0)

    for d in (0, 1):
        cols = slice(128 * d, 128 * d + 128)
        gd[:, cols] = gacc[d, :, 0:128].astype(jnp.bfloat16)
        gg[:, cols] = gacc[d, :, 128:256].astype(jnp.bfloat16)
        gu[:, cols] = gacc[d, :, 256:384].astype(jnp.bfloat16)
        for s in range(3):
            for k in range(len(PARTS)):
                rs_copy(d, s, k).wait_send()
                ag_copy(d, s, k, (r + NR - s) % NR if d == 0 else (r + s) % NR).wait_send()


def experts(tokens, meta, wg, wu, wd):
    dma = pltpu.SemaphoreType.DMA
    vm = pltpu.VMEM
    n = len(PARTS)
    return pl.pallas_call(
        expert_kernel,
        out_shape=(jax.ShapeDtypeStruct((NY * TOKS, D), jnp.bfloat16),)
        + (jax.ShapeDtypeStruct((D, H), jnp.bfloat16),) * 3,
        in_specs=[pl.BlockSpec(memory_space=pltpu.VMEM)] * 5,
        out_specs=(pl.BlockSpec(memory_space=pltpu.VMEM),) * 4,
        scratch_shapes=[
            vm((NR * ROWS, TOKS), jnp.bfloat16),
            vm((NR * ROWS, D), jnp.bfloat16),
            vm((NR * ROWS, D), jnp.bfloat16),
            vm((NR * ROWS, 3 * H), jnp.float32),
            vm((2, 3, ROWS, 384), jnp.bfloat16),
            vm((2, 3, ROWS, 384), jnp.bfloat16),
            vm((2, NR * ROWS, 384), jnp.bfloat16),
            vm((2, D, 256), jnp.bfloat16),
            vm((NR * ROWS, D), jnp.float32),
            vm((2, D, 384), jnp.float32),
            dma((2, 3, n)), dma((2, 3, n)), dma((2, 3, n)), dma((2, 3, n)),
        ],
        compiler_params=pltpu.CompilerParams(
            collective_id=1, has_side_effects=True, vmem_limit_bytes=VMEM_LIMIT
        ),
    )(tokens, meta, wg, wu, wd)


def return_kernel(t_ref, o_ref, ysnd, yrcv, col, zsnd, zrcv,
                  y_send, y_recv, z_send, z_recv):
    me, y, z, up, down = grid_place()
    greet(me, z, up, down)
    peers = (up, down)
    sides = ((me + 1, z < NZ - 1, z > 0), (me - 1, z > 0, z < NZ - 1))

    def block(c, zz, h):
        return pl.ds(pl.multiple_of(c * TOKS + zz * TOK + h * HALF, 16), HALF)

    def first(h, zz):
        c = (y + NY - 1) % NY if h == 0 else (y + 1) % NY
        return remote(t_ref.at[block(c, zz, h), :], yrcv.at[h, 0, zz],
                      y_send.at[h, 0, zz], y_recv.at[h, 0, zz], expert=peers[h])

    def later(h, s, zz):
        return remote(ysnd.at[h, s - 1, zz], yrcv.at[h, s, zz],
                      y_send.at[h, s, zz], y_recv.at[h, s, zz], expert=peers[h])

    def start(zz, carry):
        for h in (0, 1):
            first(h, zz).start()
        return carry

    lax.fori_loop(0, NZ, start, 0)
    for s in (1, 2, 3):
        def turn(zz, carry):
            for h in (0, 1):
                c = (y + 2 * NY - 1 - s) % NY if h == 0 else (y + 1 + s) % NY
                (first(h, zz) if s == 1 else later(h, s - 1, zz)).wait_recv()
                now = (t_ref[block(c, zz, h), :].astype(jnp.float32)
                       + yrcv[h, s - 1, zz].astype(jnp.float32))
                if s < 3:
                    ysnd[h, s - 1, zz] = now.astype(jnp.bfloat16)
                    later(h, s, zz).start()
                else:
                    col[h, zz] = now
            return carry

        lax.fori_loop(0, NZ, turn, 0)

    def z_copy(side, h, zz):
        return remote(zsnd.at[side, h, zz], zrcv.at[side, h, zz],
                      z_send.at[side, h, zz], z_recv.at[side, h, zz], expert=sides[side][0])

    def slot(tau, carry):
        for h in (0, 1):
            for side in (0, 1):
                zz = tau - (NZ - 1) + z if side else NZ - 1 - tau + z
                live = (zz >= 0) if side else (zz < NZ)

                @pl.when(live & sides[side][1] & sides[side][2])
                def _():
                    z_copy(side, h, zz).wait_recv()
                    zsnd[side, h, zz] = col[h, zz] + zrcv[side, h, zz]
                    z_copy(side, h, zz).start()

                @pl.when(live & sides[side][1] & jnp.logical_not(sides[side][2]))
                def _():
                    zsnd[side, h, zz] = col[h, zz]
                    z_copy(side, h, zz).start()

        return carry

    lax.fori_loop(0, NZ - 1, slot, 0)

    for h in (0, 1):
        for side in (0, 1):
            @pl.when(sides[side][2])
            def _():
                z_copy(side, h, z).wait_recv()
                col[h, z] = col[h, z] + zrcv[side, h, z]

        o_ref[h * HALF:h * HALF + HALF, :] = col[h, z].astype(jnp.bfloat16)

    def finish(zz, carry):
        for h in (0, 1):
            first(h, zz).wait_send()
            for s in (1, 2):
                later(h, s, zz).wait_send()

            @pl.when(zz > z)
            def _():
                z_copy(0, h, zz).wait_send()

            @pl.when(zz < z)
            def _():
                z_copy(1, h, zz).wait_send()

        return carry

    lax.fori_loop(0, NZ, finish, 0)


def home(table):
    dma = pltpu.SemaphoreType.DMA
    vm = pltpu.VMEM
    return pl.pallas_call(
        return_kernel,
        out_shape=jax.ShapeDtypeStruct((TOK, D), jnp.bfloat16),
        in_specs=[pl.BlockSpec(memory_space=pltpu.VMEM)],
        out_specs=pl.BlockSpec(memory_space=pltpu.VMEM),
        scratch_shapes=[
            vm((2, 2, NZ, HALF, D), jnp.bfloat16),
            vm((2, 3, NZ, HALF, D), jnp.bfloat16),
            vm((2, NZ, HALF, D), jnp.float32),
            vm((2, 2, NZ, HALF, D), jnp.float32),
            vm((2, 2, NZ, HALF, D), jnp.float32),
            dma((2, 3, NZ)), dma((2, 3, NZ)), dma((2, 2, NZ)), dma((2, 2, NZ)),
        ],
        compiler_params=pltpu.CompilerParams(
            collective_id=2, has_side_effects=True, vmem_limit_bytes=32 * 1024 * 1024
        ),
    )(table)


def shifted(value, axis, steps):
    count = lax.axis_size(axis)
    first, last = (max(0, -steps), min(count, count - steps))
    return lax.ppermute(value, axis, [(source, source + steps) for source in range(first, last)])


def table_of(routes, weights):
    chosen = routes.T[None] == jnp.arange(EXPERTS, dtype=jnp.int32)[:, None, None]
    named = jnp.sum(chosen.astype(jnp.float32), axis=1)
    weight = jnp.sum(jnp.where(chosen, weights.T[None], 0.0), axis=1)
    earlier = (jnp.arange(TOK)[:, None] < jnp.arange(TOK)[None, :]).astype(jnp.bfloat16)
    slot = jnp.dot(named.astype(jnp.bfloat16), earlier, preferred_element_type=jnp.float32)
    slot = jnp.where(named > 0.0, slot, -1.0)
    both = jnp.concatenate([slot, weight], axis=0)
    return jnp.concatenate([both, both], axis=1)


def per_device(token_grads, routing, gate_weights, layer_inputs, w_gate, w_up, w_down):
    block = jnp.concatenate([layer_inputs[0], token_grads[0]], axis=1)
    meta = table_of(routing[0], gate_weights[0])
    tokens, metas = all_tokens(block, meta)
    table, grad_gate, grad_up, grad_down = experts(tokens, metas, w_gate[0], w_up[0], w_down[0])
    upstream = shifted(home(table)[None], "section", -1)
    return (upstream, grad_gate[None], grad_up[None], grad_down[None])


def solution(mesh):
    placed = (
        P("section", "expert", "replica"),
        P("section", "expert", None),
        P("section", "expert", None),
        P("section", "expert", "replica"),
        P("section", "replica", "expert"),
        P("section", "replica", "expert"),
        P("section", "replica", "expert"),
    )
    return jax.shard_map(
        per_device,
        mesh=mesh,
        in_specs=placed,
        out_specs=(
            P("section", "expert", "replica"),
            P("section", "replica", "expert"),
            P("section", "replica", "expert"),
            P("section", "replica", "expert"),
        ),
        check_vma=False,
    )
```

```python
import jax
import jax.numpy as jnp
from jax import lax
from jax.experimental import pallas as pl
from jax.experimental.pallas import tpu as pltpu
from jax.sharding import PartitionSpec as P

MESH = pl.DeviceIdType.MESH
SHARES = 4
NY, NZ, NR = 4, 8, 4
EXPERTS = 8
TOK = 64
CAP = 34
D = 896
H = 256
ROWS = NZ * CAP
TOKS = NZ * TOK
HALF = TOK // 2
PIECE, REST = 64, 16
COLUMN = (0, 1, 3, 2)
VMEM_LIMIT = 60 * 1024 * 1024


def remote(src, dst, send_sem, recv_sem, **where):
    return pltpu.make_async_remote_copy(
        src_ref=src, dst_ref=dst, send_sem=send_sem, recv_sem=recv_sem,
        device_id=where, device_id_type=MESH,
    )


def rows_of(ref, start, size):
    return ref.at[pl.ds(pl.multiple_of(start, 16), size), :]


def grid_place():
    me = lax.axis_index("expert")
    y, z = me // NZ, me % NZ
    return me, y, z, (y + 1) % NY * NZ + z, (y + NY - 1) % NY * NZ + z


def over_rows(left, right):
    return lax.dot_general(
        left, right, (((0,), (0,)), ((), ())), preferred_element_type=jnp.float32
    )


def over_cols(left, right):
    return lax.dot_general(
        left, right, (((1,), (1,)), ((), ())), preferred_element_type=jnp.float32
    )


def kernel(b_ref, m_ref, wg, wu, wd, o_ref, gg, gu, gd,
           ball, mall, pick, picks, xs, gs, part, snd, rcv, snd_rest, rcv_rest, act, wcat, gacc,
           bsnd, brcv, total, zsnd, zrcv, own_sem,
           zb_send, zb_recv, zm_send, zm_recv, yb_send, yb_recv, ym_send, ym_recv,
           fb_send, fb_recv, fm_send, fm_recv, rs_send, rs_recv, ag_send, ag_recv,
           b_send, b_recv, z_send, z_recv):
    me, y, z, up, down = grid_place()
    r = lax.axis_index("replica")
    peers = (up, down)
    rings = ((r + 1) % NR, (r + NR - 1) % NR)
    far_off = (y + 2) % NY * NZ + z
    sides = ((me + 1, z < NZ - 1, z > 0), (me - 1, z > 0, z < NZ - 1))

    barrier = pltpu.get_barrier_semaphore()
    for peer in (up, down, far_off):
        pl.semaphore_signal(barrier, inc=1, device_id={"expert": peer}, device_id_type=MESH)
    for peer in rings:
        pl.semaphore_signal(barrier, inc=1, device_id={"replica": peer}, device_id_type=MESH)
    for side in (0, 1):
        @pl.when(sides[side][1])
        def _():
            pl.semaphore_signal(barrier, inc=1, device_id={"expert": sides[side][0]}, device_id_type=MESH)

    pl.semaphore_wait(barrier, 7 - (NZ - z) // NZ - (z + 1) // NZ)

    own_b = pltpu.make_async_copy(b_ref, rows_of(ball, me * TOK, TOK), own_sem.at[0])
    own_m = pltpu.make_async_copy(m_ref, mall.at[me], own_sem.at[1])
    own_b.start()
    own_m.start()
    own_b.wait()
    own_m.wait()

    def z_copies(side, t, zz):
        at = y * NZ + zz
        to = sides[side][0]
        b = rows_of(ball, at * TOK, TOK)
        return (
            remote(b, b, zb_send.at[side, t], zb_recv.at[side, t], expert=to),
            remote(mall.at[at], mall.at[at], zm_send.at[side, t], zm_recv.at[side, t], expert=to),
        )

    def y_copies(way, col, zz):
        at = col * NZ + zz
        b = rows_of(ball, at * TOK, TOK)
        return (
            remote(b, b, yb_send.at[way, zz], yb_recv.at[way, zz], expert=peers[way]),
            remote(mall.at[at], mall.at[at], ym_send.at[way, zz], ym_recv.at[way, zz], expert=peers[way]),
        )

    def far_copy(way, col, zz):
        b = rows_of(ball, (col * NZ + zz) * TOK + way * HALF, HALF)
        return remote(b, b, fb_send.at[way, zz], fb_recv.at[way, zz], expert=peers[way])

    def far_meta(col, zz):
        at = col * NZ + zz
        return remote(mall.at[at], mall.at[at], fm_send.at[zz], fm_recv.at[zz], expert=up)

    came_up, came_down, far = (y + NY - 1) % NY, (y + 1) % NY, (y + 2) % NY

    def along(t, carry):
        for side in (0, 1):
            zz = z + t if side else z - t
            inside = (zz >= 0) & (zz < NZ)

            @pl.when(inside & (t > 0))
            def _():
                for c in z_copies(side, t - 1, zz):
                    c.wait_recv()

            @pl.when(inside & sides[side][1])
            def _():
                for c in z_copies(side, t, zz):
                    c.start()

            @pl.when(inside & ((t > 0) if side else (t >= 0)))
            def _():
                for way in (0, 1):
                    for c in y_copies(way, y, zz):
                        c.start()

        return carry

    lax.fori_loop(0, NZ, along, 0)

    def round_y(t, carry):
        for side in (0, 1):
            zz = z + t if side else z - t

            @pl.when((zz >= 0) & (zz < NZ) & ((t > 0) if side else (t >= 0)))
            def _():
                for c in y_copies(0, came_up, zz):
                    c.wait_recv()
                far_copy(0, came_up, zz).start()
                far_meta(came_up, zz).start()
                for c in y_copies(1, came_down, zz):
                    c.wait_recv()
                far_copy(1, came_down, zz).start()

        return carry

    def round_far(zz, carry):
        for way in (0, 1):
            far_copy(way, far, zz).wait_recv()
        far_meta(far, zz).wait_recv()
        return carry

    lane = lax.broadcasted_iota(jnp.int32, (1, 128), 1)
    first = lane < TOK
    row = lax.broadcasted_iota(jnp.int32, (ROWS, 128), 0).astype(jnp.float32)
    which = lax.broadcasted_iota(jnp.int32, (NZ, EXPERTS, 128), 1)

    def choose(to, at, c, e):
        meta = mall[pl.ds(c * NZ, NZ)]
        slots = jnp.sum(jnp.where(which == e, meta[:, 0:8, :], 0.0), axis=1)
        scale = jnp.sum(jnp.where(which == e, meta[:, 8:16, :], 0.0), axis=1)
        weight = jnp.zeros((ROWS, 128), jnp.float32)
        for p in range(NZ // 2):
            slot = jnp.where(first, slots[2 * p:2 * p + 1], slots[2 * p + 1:2 * p + 2])
            w = jnp.where(first, scale[2 * p:2 * p + 1], scale[2 * p + 1:2 * p + 2])
            base = jnp.where(first, float(CAP * 2 * p), float(CAP * (2 * p + 1)))
            hit = row == jnp.where(slot >= 0.0, slot + base, -1.0)
            weight = weight + jnp.where(hit, w, 0.0)
            to[pl.ds(pl.multiple_of(at, 16), ROWS), 128 * p:128 * p + 128] = jnp.where(hit, 1.0, 0.0).astype(jnp.bfloat16)
        return jnp.sum(weight, axis=1, keepdims=True)

    def column(g):
        return (y + COLUMN[g]) % NY

    def column_rows(g):
        return pl.ds(pl.multiple_of(column(g) * ROWS, 16), ROWS)

    def products(g):
        c = column(g)
        rows = column_rows(g)
        toks = pl.ds(pl.multiple_of(c * TOKS, 16), TOKS)
        weight = choose(pick, c * ROWS, c, me // SHARES)
        sel = pick[rows, :]
        x = jnp.dot(sel, ball[toks, 0:D], preferred_element_type=jnp.float32).astype(jnp.bfloat16)
        xs[rows, :] = x
        gr = jnp.dot(sel, ball[toks, D:2 * D], preferred_element_type=jnp.float32)
        gr = (gr * weight).astype(jnp.bfloat16)
        gs[rows, :] = gr
        part[rows, 0:256] = jnp.dot(x, wg[...], preferred_element_type=jnp.float32)
        part[rows, 256:512] = jnp.dot(x, wu[...], preferred_element_type=jnp.float32)
        part[rows, 512:768] = jnp.dot(gr, wd[...], preferred_element_type=jnp.float32)

    def piece(g, o):
        if g < NY:
            return pl.ds(pl.multiple_of(column(g) * ROWS + o * PIECE, 16), PIECE)
        return pl.ds(pl.multiple_of(o * ROWS + NR * PIECE, 16), REST)

    def out_of(g):
        return (snd.at[g], rcv.at[g]) if g < NY else (snd_rest, rcv_rest)

    def rs_copy(g, d, s):
        a, b = out_of(g)
        return remote(a.at[d, s], b.at[d, s], rs_send.at[g, d, s], rs_recv.at[g, d, s], replica=rings[d])

    def stage(g, s):
        for d in (0, 1):
            o = (r + NR - 1 - s) % NR if d == 0 else (r + 1 + s) % NR
            rows = piece(g, o)
            a, b = out_of(g)
            if s:
                rs_copy(g, d, s - 1).wait_recv()
            for kind in range(3):
                mine = part[rows, 256 * kind + 128 * d:256 * kind + 128 * d + 128]
                cols = slice(128 * kind, 128 * kind + 128)
                if s:
                    mine = mine + b[d, s - 1, :, cols].astype(jnp.float32)
                a[d, s, :, cols] = mine.astype(jnp.bfloat16)
            rs_copy(g, d, s).start()

    def ag_copy(g, d, s):
        there = act.at[d, piece(g, (r + NR - s) % NR if d == 0 else (r + s) % NR), :]
        return remote(there, there, ag_send.at[g, d, s], ag_recv.at[g, d, s], replica=rings[d])

    def arrived(g, d, s):
        there = act.at[d, piece(g, (r + NR - 1 - s) % NR if d == 0 else (r + 1 + s) % NR), :]
        return remote(there, there, ag_send.at[g, d, s], ag_recv.at[g, d, s], replica=rings[d])

    def final(g):
        for d in (0, 1):
            rs_copy(g, d, 2).wait_recv()
            rows = piece(g, r)
            b = out_of(g)[1]
            gate, upp, dh = [
                part[rows, 256 * kind + 128 * d:256 * kind + 128 * d + 128]
                + b[d, 2, :, 128 * kind:128 * kind + 128].astype(jnp.float32)
                for kind in range(3)
            ]
            sg = jax.nn.sigmoid(gate)
            a = gate * sg
            act[d, rows, 0:128] = (a * upp).astype(jnp.bfloat16)
            act[d, rows, 128:256] = (dh * upp * (sg * (1.0 + gate * (1.0 - sg)))).astype(jnp.bfloat16)
            act[d, rows, 256:384] = (dh * a).astype(jnp.bfloat16)
            ag_copy(g, d, 0).start()

    def onward(g, s):
        for d in (0, 1):
            arrived(g, d, s - 1).wait_recv()
            if s < NR - 1:
                ag_copy(g, d, s).start()

    def back_copy(g):
        to = (me, up, down, far_off)[g]
        return remote(bsnd.at[g], brcv.at[g], b_send.at[g], b_recv.at[g], expert=to)

    def backward(g):
        rows = column_rows(g)
        back = over_cols(act[0, rows, 128:384], wcat[0]) + over_cols(act[1, rows, 128:384], wcat[1])
        if g:
            bsnd[g] = back.astype(jnp.bfloat16)
            back_copy(g).start()
        else:
            brcv[0] = back.astype(jnp.bfloat16)

    def weights(g, fresh):
        rows = column_rows(g)
        for d in (0, 1):
            up_down = over_rows(xs[rows, :], act[d, rows, 128:384])
            hid = over_rows(gs[rows, :], act[d, rows, 0:128])
            if fresh:
                gacc[d, :, 128:384] = up_down
                gacc[d, :, 0:128] = hid
            else:
                gacc[d, :, 128:384] = gacc[d, :, 128:384] + up_down
                gacc[d, :, 0:128] = gacc[d, :, 0:128] + hid

    def collect(g, fresh):
        if g:
            back_copy(g).wait_recv()
        mine = over_rows(picks[g], brcv[g])
        total[...] = mine if fresh else total[...] + mine

    products(0)
    stage(0, 0)
    for d in (0, 1):
        wcat[d, :, 0:128] = wg[:, 128 * d:128 * d + 128]
        wcat[d, :, 128:256] = wu[:, 128 * d:128 * d + 128]
    lax.fori_loop(0, NZ, round_y, 0)
    stage(0, 1)
    products(1)
    stage(1, 0)
    products(2)
    stage(2, 0)
    stage(0, 2)
    lax.fori_loop(0, NZ, round_far, 0)
    products(3)
    stage(4, 0)
    stage(3, 0)
    for g in (1, 2, 4, 3):
        stage(g, 1)
    for g in range(NY):
        choose(picks.at[g], 0, y, (y + (0, 3, 1, 2)[g]) % NY * 2 + z // SHARES)
    for g in (1, 2, 4, 3):
        stage(g, 2)
    final(1)
    final(2)
    final(4)
    onward(1, 1)
    final(3)
    onward(2, 1)
    onward(4, 1)
    onward(1, 2)
    final(0)
    onward(3, 1)
    onward(2, 2)
    onward(4, 2)
    onward(4, 3)
    onward(1, 3)
    backward(1)
    onward(3, 2)
    onward(0, 1)
    weights(1, True)
    onward(2, 3)
    backward(2)
    onward(0, 2)
    weights(2, False)
    onward(3, 3)
    backward(3)
    weights(3, False)
    collect(1, True)
    collect(2, False)
    onward(0, 3)
    backward(0)
    collect(0, False)
    collect(3, False)

    def z_copy(side, h, zz):
        return remote(zsnd.at[side, h, zz], zrcv.at[side, h, zz],
                      z_send.at[side, h, zz], z_recv.at[side, h, zz], expert=sides[side][0])

    def of_group(h, zz):
        return total[pl.ds(pl.multiple_of(zz * TOK + h * HALF, 16), HALF), :]

    def slot(tau, carry):
        for h in (0, 1):
            for side in (0, 1):
                zz = tau - (NZ - 1) + z if side else NZ - 1 - tau + z
                live = (zz >= 0) if side else (zz < NZ)

                @pl.when(live & sides[side][1] & sides[side][2])
                def _():
                    z_copy(side, h, zz).wait_recv()
                    zsnd[side, h, zz] = (of_group(h, zz) + zrcv[side, h, zz].astype(jnp.float32)).astype(jnp.bfloat16)
                    z_copy(side, h, zz).start()

                @pl.when(live & sides[side][1] & jnp.logical_not(sides[side][2]))
                def _():
                    zsnd[side, h, zz] = of_group(h, zz).astype(jnp.bfloat16)
                    z_copy(side, h, zz).start()

        return carry

    lax.fori_loop(0, 1, slot, 0)
    weights(0, False)
    lax.fori_loop(1, NZ - 1, slot, 0)
    for h in (0, 1):
        at = pl.ds(pl.multiple_of(z * TOK + h * HALF, 16), HALF)
        for side in (0, 1):
            @pl.when(sides[side][2])
            def _():
                z_copy(side, h, z).wait_recv()
                total[at, :] = total[at, :] + zrcv[side, h, z].astype(jnp.float32)

        o_ref[h * HALF:h * HALF + HALF, :] = total[at, :].astype(jnp.bfloat16)

    for d in (0, 1):
        cols = slice(128 * d, 128 * d + 128)
        gd[:, cols] = gacc[d, :, 0:128].astype(jnp.bfloat16)
        gg[:, cols] = gacc[d, :, 128:256].astype(jnp.bfloat16)
        gu[:, cols] = gacc[d, :, 256:384].astype(jnp.bfloat16)

    def finish(zz, carry):
        for way in (0, 1):
            far_copy(way, (came_up, came_down)[way], zz).wait_send()
            for c in y_copies(way, y, zz):
                c.wait_send()
        far_meta(came_up, zz).wait_send()
        for side in (0, 1):
            src = z + zz if side else z - zz

            @pl.when((src >= 0) & (src < NZ) & sides[side][1])
            def _():
                for c in z_copies(side, zz, src):
                    c.wait_send()

        for h in (0, 1):
            @pl.when(zz > z)
            def _():
                z_copy(0, h, zz).wait_send()

            @pl.when(zz < z)
            def _():
                z_copy(1, h, zz).wait_send()

        return carry

    lax.fori_loop(0, NZ, finish, 0)
    for g in range(NY + 1):
        for d in (0, 1):
            for s in range(NR - 1):
                rs_copy(g, d, s).wait_send()
                ag_copy(g, d, s).wait_send()
    for g in (1, 2, 3):
        back_copy(g).wait_send()


def layer(tokens, meta, wg, wu, wd):
    dma = pltpu.SemaphoreType.DMA
    vm = pltpu.VMEM
    bf, f32 = jnp.bfloat16, jnp.float32
    rows = NR * ROWS
    return pl.pallas_call(
        kernel,
        out_shape=(jax.ShapeDtypeStruct((TOK, D), bf),) + (jax.ShapeDtypeStruct((D, H), bf),) * 3,
        in_specs=[pl.BlockSpec(memory_space=pltpu.VMEM)] * 5,
        out_specs=(pl.BlockSpec(memory_space=pltpu.VMEM),) * 4,
        scratch_shapes=[
            vm((NY * TOKS, 2 * D), bf), vm((NY * NZ, 16, 128), f32),
            vm((rows, TOKS), bf), vm((NY, ROWS, TOKS), bf),
            vm((rows, D), bf), vm((rows, D), bf), vm((rows, 3 * H), f32),
            vm((NY, 2, 3, PIECE, 384), bf), vm((NY, 2, 3, PIECE, 384), bf),
            vm((2, 3, REST, 384), bf), vm((2, 3, REST, 384), bf),
            vm((2, rows, 384), bf), vm((2, D, 256), bf), vm((2, D, 384), f32),
            vm((NY, ROWS, D), bf), vm((NY, ROWS, D), bf), vm((TOKS, D), f32),
            vm((2, 2, NZ, HALF, D), bf), vm((2, 2, NZ, HALF, D), bf),
            dma((2,)),
        ] + [dma((2, NZ))] * 10 + [dma((NZ,))] * 2 + [dma((NY + 1, 2, 3))] * 4
        + [dma((NY,))] * 2 + [dma((2, 2, NZ))] * 2,
        compiler_params=pltpu.CompilerParams(
            collective_id=0, has_side_effects=True, vmem_limit_bytes=VMEM_LIMIT
        ),
    )(tokens, meta, wg, wu, wd)


def shifted(value, axis, steps):
    count = lax.axis_size(axis)
    first, last = (max(0, -steps), min(count, count - steps))
    return lax.ppermute(value, axis, [(source, source + steps) for source in range(first, last)])


def table_of(routes, weights):
    chosen = routes.T[None] == jnp.arange(EXPERTS, dtype=jnp.int32)[:, None, None]
    named = jnp.sum(chosen.astype(jnp.float32), axis=1)
    weight = jnp.sum(jnp.where(chosen, weights.T[None], 0.0), axis=1)
    earlier = (jnp.arange(TOK)[:, None] < jnp.arange(TOK)[None, :]).astype(jnp.bfloat16)
    slot = jnp.dot(named.astype(jnp.bfloat16), earlier, preferred_element_type=jnp.float32)
    slot = jnp.where(named > 0.0, slot, -1.0)
    both = jnp.concatenate([slot, weight], axis=0)
    return jnp.concatenate([both, both], axis=1)


def per_device(token_grads, routing, gate_weights, layer_inputs, w_gate, w_up, w_down):
    block = jnp.concatenate([layer_inputs[0], token_grads[0]], axis=1)
    meta = table_of(routing[0], gate_weights[0])
    boundary, grad_gate, grad_up, grad_down = layer(block, meta, w_gate[0], w_up[0], w_down[0])
    upstream = shifted(boundary[None], "section", -1)
    return (upstream, grad_gate[None], grad_up[None], grad_down[None])


def solution(mesh):
    placed = (
        P("section", "expert", "replica"),
        P("section", "expert", None),
        P("section", "expert", None),
        P("section", "expert", "replica"),
        P("section", "replica", "expert"),
        P("section", "replica", "expert"),
        P("section", "replica", "expert"),
    )
    return jax.shard_map(
        per_device,
        mesh=mesh,
        in_specs=placed,
        out_specs=(
            P("section", "expert", "replica"),
            P("section", "replica", "expert"),
            P("section", "replica", "expert"),
            P("section", "replica", "expert"),
        ),
        check_vma=False,
    )
```

```python
import jax
import jax.numpy as jnp
from jax import lax
from jax.experimental import pallas as pl
from jax.experimental.pallas import tpu as pltpu
from jax.sharding import PartitionSpec as P

MESH = pl.DeviceIdType.MESH
SHARES = 4
NY, NZ, NR = 4, 8, 4
EXPERTS = 8
TOK = 64
CAP = 34
D = 896
H = 256
ROWS = NZ * CAP
TOKS = NZ * TOK
HALF = TOK // 2
PIECE, REST = 64, 16
COLUMN = (0, 1, 3, 2)
GROUPS = ((0, 0, 32), (1, 0, 64), (2, 0, 64), (3, 0, 64), None, (0, 32, 32))
NS = 8
VMEM_LIMIT = 60 * 1024 * 1024


def remote(src, dst, send_sem, recv_sem, **where):
    return pltpu.make_async_remote_copy(
        src_ref=src, dst_ref=dst, send_sem=send_sem, recv_sem=recv_sem,
        device_id=where, device_id_type=MESH,
    )


def rows_of(ref, start, size):
    return ref.at[pl.ds(pl.multiple_of(start, 16), size), :]


def grid_place():
    me = lax.axis_index("expert")
    y, z = me // NZ, me % NZ
    return me, y, z, (y + 1) % NY * NZ + z, (y + NY - 1) % NY * NZ + z


def over_rows(left, right):
    return lax.dot_general(
        left, right, (((0,), (0,)), ((), ())), preferred_element_type=jnp.float32
    )


def over_cols(left, right):
    return lax.dot_general(
        left, right, (((1,), (1,)), ((), ())), preferred_element_type=jnp.float32
    )


def kernel(b_ref, m_ref, wg, wu, wd, o_ref, gg, gu, gd,
           ball, mall, pick, picks, xs, gs, part, snd, rcv, snd_rest, rcv_rest, act, wcat, gacc,
           bsnd, brcv, total, zsnd, zrcv, edge, own_sem,
           zb_send, zb_recv, zm_send, zm_recv, yb_send, yb_recv, ym_send, ym_recv,
           fb_send, fb_recv, fm_send, fm_recv, rs_send, rs_recv, ag_send, ag_recv,
           b_send, b_recv, z_send, z_recv, s_send, s_recv):
    me, y, z, up, down = grid_place()
    r = lax.axis_index("replica")
    sec = lax.axis_index("section")
    peers = (up, down)
    rings = ((r + 1) % NR, (r + NR - 1) % NR)
    far_off = (y + 2) % NY * NZ + z
    sides = ((me + 1, z < NZ - 1, z > 0), (me - 1, z > 0, z < NZ - 1))

    barrier = pltpu.get_barrier_semaphore()
    for peer in (up, down, far_off):
        pl.semaphore_signal(barrier, inc=1, device_id={"expert": peer}, device_id_type=MESH)
    for peer in rings:
        pl.semaphore_signal(barrier, inc=1, device_id={"replica": peer}, device_id_type=MESH)
    for side in (0, 1):
        @pl.when(sides[side][1])
        def _():
            pl.semaphore_signal(barrier, inc=1, device_id={"expert": sides[side][0]}, device_id_type=MESH)

    for near, there in ((sec - 1, sec > 0), (sec + 1, sec < NS - 1)):
        @pl.when(there)
        def _():
            pl.semaphore_signal(barrier, inc=1, device_id={"section": near}, device_id_type=MESH)

    pl.semaphore_wait(
        barrier, 9 - (NZ - z) // NZ - (z + 1) // NZ - (NS - sec) // NS - (sec + 1) // NS
    )

    own_b = pltpu.make_async_copy(b_ref, rows_of(ball, me * TOK, TOK), own_sem.at[0])
    own_m = pltpu.make_async_copy(m_ref, mall.at[me], own_sem.at[1])
    own_b.start()
    own_m.start()
    own_b.wait()
    own_m.wait()

    def half(at, h):
        return rows_of(ball, at * TOK + h * HALF, HALF)

    def z_half(side, t, zz, h):
        b = half(y * NZ + zz, h)
        return remote(b, b, zb_send.at[side, t, h], zb_recv.at[side, t, h], expert=sides[side][0])

    def z_meta(side, t, zz):
        m = mall.at[y * NZ + zz]
        return remote(m, m, zm_send.at[side, t], zm_recv.at[side, t], expert=sides[side][0])

    def y_half(way, col, zz, h):
        b = half(col * NZ + zz, h)
        return remote(b, b, yb_send.at[way, zz, h], yb_recv.at[way, zz, h], expert=peers[way])

    def y_meta(way, col, zz):
        m = mall.at[col * NZ + zz]
        return remote(m, m, ym_send.at[way, zz], ym_recv.at[way, zz], expert=peers[way])

    def far_copy(way, col, zz):
        b = rows_of(ball, (col * NZ + zz) * TOK + way * HALF, HALF)
        return remote(b, b, fb_send.at[way, zz], fb_recv.at[way, zz], expert=peers[way])

    def far_meta(col, zz):
        at = col * NZ + zz
        return remote(mall.at[at], mall.at[at], fm_send.at[zz], fm_recv.at[zz], expert=up)

    came_up, came_down, far = (y + NY - 1) % NY, (y + 1) % NY, (y + 2) % NY

    def along(t, carry):
        for h in (0, 1):
            for side in (0, 1):
                zz = z + t if side else z - t
                inside = (zz >= 0) & (zz < NZ)

                @pl.when(inside & (t > 0))
                def _():
                    if h == 0:
                        z_meta(side, t - 1, zz).wait_recv()
                    z_half(side, t - 1, zz, h).wait_recv()

                @pl.when(inside & sides[side][1])
                def _():
                    if h == 0:
                        z_meta(side, t, zz).start()
                    z_half(side, t, zz, h).start()

                @pl.when(inside & ((t > 0) if side else (t >= 0)))
                def _():
                    for way in (0, 1):
                        if h == 0:
                            y_meta(way, y, zz).start()
                        y_half(way, y, zz, h).start()

        return carry

    lax.fori_loop(0, NZ, along, 0)

    def round_y(t, carry):
        for side in (0, 1):
            zz = z + t if side else z - t

            @pl.when((zz >= 0) & (zz < NZ) & ((t > 0) if side else (t >= 0)))
            def _():
                y_meta(0, came_up, zz).wait_recv()
                far_meta(came_up, zz).start()
                y_half(0, came_up, zz, 0).wait_recv()
                far_copy(0, came_up, zz).start()
                y_half(1, came_down, zz, 1).wait_recv()
                far_copy(1, came_down, zz).start()

        return carry

    def round_rest(zz, carry):
        y_half(0, came_up, zz, 1).wait_recv()
        y_meta(1, came_down, zz).wait_recv()
        y_half(1, came_down, zz, 0).wait_recv()
        return carry

    def round_far(zz, carry):
        for way in (0, 1):
            far_copy(way, far, zz).wait_recv()
        far_meta(far, zz).wait_recv()
        return carry

    lane = lax.broadcasted_iota(jnp.int32, (1, 128), 1)
    first = lane < TOK
    row = lax.broadcasted_iota(jnp.int32, (ROWS, 128), 0).astype(jnp.float32)
    which = lax.broadcasted_iota(jnp.int32, (NZ, EXPERTS, 128), 1)

    def choose(to, at, c, e):
        meta = mall[pl.ds(c * NZ, NZ)]
        slots = jnp.sum(jnp.where(which == e, meta[:, 0:8, :], 0.0), axis=1)
        scale = jnp.sum(jnp.where(which == e, meta[:, 8:16, :], 0.0), axis=1)
        weight = jnp.zeros((ROWS, 128), jnp.float32)
        for p in range(NZ // 2):
            slot = jnp.where(first, slots[2 * p:2 * p + 1], slots[2 * p + 1:2 * p + 2])
            w = jnp.where(first, scale[2 * p:2 * p + 1], scale[2 * p + 1:2 * p + 2])
            base = jnp.where(first, float(CAP * 2 * p), float(CAP * (2 * p + 1)))
            hit = row == jnp.where(slot >= 0.0, slot + base, -1.0)
            weight = weight + jnp.where(hit, w, 0.0)
            to[pl.ds(pl.multiple_of(at, 16), ROWS), 128 * p:128 * p + 128] = jnp.where(hit, 1.0, 0.0).astype(jnp.bfloat16)
        return jnp.sum(weight, axis=1, keepdims=True)

    def column(g):
        return (y + COLUMN[g]) % NY

    def column_rows(g):
        return pl.ds(pl.multiple_of(column(g) * ROWS, 16), ROWS)

    def products(g):
        c = column(g)
        rows = column_rows(g)
        toks = pl.ds(pl.multiple_of(c * TOKS, 16), TOKS)
        weight = choose(pick, c * ROWS, c, me // SHARES)
        sel = pick[rows, :]
        x = jnp.dot(sel, ball[toks, 0:D], preferred_element_type=jnp.float32).astype(jnp.bfloat16)
        xs[rows, :] = x
        gr = jnp.dot(sel, ball[toks, D:2 * D], preferred_element_type=jnp.float32)
        gr = (gr * weight).astype(jnp.bfloat16)
        gs[rows, :] = gr
        part[rows, 0:256] = jnp.dot(x, wg[...], preferred_element_type=jnp.float32)
        part[rows, 256:512] = jnp.dot(x, wu[...], preferred_element_type=jnp.float32)
        part[rows, 512:768] = jnp.dot(gr, wd[...], preferred_element_type=jnp.float32)

    def piece(g, o):
        if g == NY:
            return pl.ds(pl.multiple_of(o * ROWS + NR * PIECE, 16), REST)
        c, at, size = GROUPS[g]
        return pl.ds(pl.multiple_of(column(c) * ROWS + o * PIECE + at, 16), size)

    def out_of(g, d, s):
        if g == NY:
            return snd_rest.at[d, s], rcv_rest.at[d, s]
        c, at, size = GROUPS[g]
        return snd.at[c, d, s, at:at + size], rcv.at[c, d, s, at:at + size]

    def rs_copy(g, d, s):
        a, b = out_of(g, d, s)
        return remote(a, b, rs_send.at[g, d, s], rs_recv.at[g, d, s], replica=rings[d])

    def stage(g, s):
        for d in (0, 1):
            o = (r + NR - 1 - s) % NR if d == 0 else (r + 1 + s) % NR
            rows = piece(g, o)
            a = out_of(g, d, s)[0]
            if s:
                b = out_of(g, d, s - 1)[1]
                rs_copy(g, d, s - 1).wait_recv()
            for kind in range(3):
                mine = part[rows, 256 * kind + 128 * d:256 * kind + 128 * d + 128]
                cols = slice(128 * kind, 128 * kind + 128)
                if s:
                    mine = mine + b[:, cols].astype(jnp.float32)
                a[:, cols] = mine.astype(jnp.bfloat16)
            rs_copy(g, d, s).start()

    def ag_copy(g, d, s):
        there = act.at[d, piece(g, (r + NR - s) % NR if d == 0 else (r + s) % NR), :]
        return remote(there, there, ag_send.at[g, d, s], ag_recv.at[g, d, s], replica=rings[d])

    def arrived(g, d, s):
        there = act.at[d, piece(g, (r + NR - 1 - s) % NR if d == 0 else (r + 1 + s) % NR), :]
        return remote(there, there, ag_send.at[g, d, s], ag_recv.at[g, d, s], replica=rings[d])

    def final(g):
        for d in (0, 1):
            rs_copy(g, d, 2).wait_recv()
            rows = piece(g, r)
            b = out_of(g, d, 2)[1]
            gate, upp, dh = [
                part[rows, 256 * kind + 128 * d:256 * kind + 128 * d + 128]
                + b[:, 128 * kind:128 * kind + 128].astype(jnp.float32)
                for kind in range(3)
            ]
            sg = jax.nn.sigmoid(gate)
            a = gate * sg
            act[d, rows, 0:128] = (a * upp).astype(jnp.bfloat16)
            act[d, rows, 128:256] = (dh * upp * (sg * (1.0 + gate * (1.0 - sg)))).astype(jnp.bfloat16)
            act[d, rows, 256:384] = (dh * a).astype(jnp.bfloat16)
            ag_copy(g, d, 0).start()

    def onward(g, s):
        for d in (0, 1):
            arrived(g, d, s - 1).wait_recv()
            if s < NR - 1:
                ag_copy(g, d, s).start()

    def back_copy(g):
        to = (me, up, down, far_off)[g]
        return remote(bsnd.at[g], brcv.at[g], b_send.at[g], b_recv.at[g], expert=to)

    def backward(g):
        rows = column_rows(g)
        back = over_cols(act[0, rows, 128:384], wcat[0]) + over_cols(act[1, rows, 128:384], wcat[1])
        if g:
            bsnd[g] = back.astype(jnp.bfloat16)
            back_copy(g).start()
        else:
            brcv[0] = back.astype(jnp.bfloat16)

    def weights(g, fresh):
        rows = column_rows(g)
        for d in (0, 1):
            up_down = over_rows(xs[rows, :], act[d, rows, 128:384])
            hid = over_rows(gs[rows, :], act[d, rows, 0:128])
            if fresh:
                gacc[d, :, 128:384] = up_down
                gacc[d, :, 0:128] = hid
            else:
                gacc[d, :, 128:384] = gacc[d, :, 128:384] + up_down
                gacc[d, :, 0:128] = gacc[d, :, 0:128] + hid

    def collect(g, fresh):
        if g:
            back_copy(g).wait_recv()
        mine = over_rows(picks[g], brcv[g])
        total[...] = mine if fresh else total[...] + mine

    products(0)
    stage(0, 0)
    stage(5, 0)
    lax.fori_loop(0, NZ, round_y, 0)
    lax.fori_loop(0, NZ, round_rest, 0)
    stage(0, 1)
    stage(5, 1)
    products(1)
    stage(1, 0)
    products(2)
    stage(2, 0)
    stage(0, 2)
    stage(5, 2)
    lax.fori_loop(0, NZ, round_far, 0)
    products(3)
    stage(4, 0)
    stage(3, 0)
    for g in (1, 2, 4, 3):
        stage(g, 1)
    for d in (0, 1):
        wcat[d, :, 0:128] = wg[:, 128 * d:128 * d + 128]
        wcat[d, :, 128:256] = wu[:, 128 * d:128 * d + 128]
    for g in range(NY):
        choose(picks.at[g], 0, y, (y + (0, 3, 1, 2)[g]) % NY * 2 + z // SHARES)
    for g in (1, 2, 4, 3):
        stage(g, 2)
    final(1)
    final(2)
    final(4)
    onward(1, 1)
    final(3)
    onward(2, 1)
    onward(4, 1)
    onward(1, 2)
    final(0)
    final(5)
    onward(3, 1)
    onward(2, 2)
    onward(4, 2)
    onward(1, 3)
    onward(0, 1)
    onward(5, 1)
    onward(3, 2)
    onward(2, 3)
    onward(4, 3)
    backward(1)
    backward(2)
    onward(0, 2)
    onward(5, 2)
    weights(1, True)
    onward(3, 3)
    backward(3)
    weights(2, False)
    weights(3, False)
    collect(1, True)
    collect(2, False)
    onward(0, 3)
    onward(5, 3)
    backward(0)
    collect(0, False)
    collect(3, False)

    def z_copy(side, h, zz):
        return remote(zsnd.at[side, h, zz], zrcv.at[side, h, zz],
                      z_send.at[side, h, zz], z_recv.at[side, h, zz], expert=sides[side][0])

    def of_group(h, zz):
        return total[pl.ds(pl.multiple_of(zz * TOK + h * HALF, 16), HALF), :]

    def slot(tau, carry):
        for h in (0, 1):
            for side in (0, 1):
                zz = tau - (NZ - 1) + z if side else NZ - 1 - tau + z
                live = (zz >= 0) if side else (zz < NZ)

                @pl.when(live & sides[side][1] & sides[side][2])
                def _():
                    z_copy(side, h, zz).wait_recv()
                    zsnd[side, h, zz] = (of_group(h, zz) + zrcv[side, h, zz].astype(jnp.float32)).astype(jnp.bfloat16)
                    z_copy(side, h, zz).start()

                @pl.when(live & sides[side][1] & jnp.logical_not(sides[side][2]))
                def _():
                    zsnd[side, h, zz] = of_group(h, zz).astype(jnp.bfloat16)
                    z_copy(side, h, zz).start()

        return carry

    lax.fori_loop(0, 1, slot, 0)
    weights(0, False)
    lax.fori_loop(1, NZ - 1, slot, 0)
    for h in (0, 1):
        at = pl.ds(pl.multiple_of(z * TOK + h * HALF, 16), HALF)
        for side in (0, 1):
            @pl.when(sides[side][2])
            def _():
                z_copy(side, h, z).wait_recv()
                total[at, :] = total[at, :] + zrcv[side, h, z].astype(jnp.float32)

        edge[h * HALF:h * HALF + HALF, :] = total[at, :].astype(jnp.bfloat16)

    def shift():
        return remote(edge, o_ref, s_send, s_recv, section=sec - 1)

    @pl.when(sec > 0)
    def _():
        shift().start()

    @pl.when(sec == NS - 1)
    def _():
        o_ref[...] = jnp.zeros_like(o_ref)

    for d in (0, 1):
        cols = slice(128 * d, 128 * d + 128)
        gd[:, cols] = gacc[d, :, 0:128].astype(jnp.bfloat16)
        gg[:, cols] = gacc[d, :, 128:256].astype(jnp.bfloat16)
        gu[:, cols] = gacc[d, :, 256:384].astype(jnp.bfloat16)

    def finish(zz, carry):
        for way in (0, 1):
            far_copy(way, (came_up, came_down)[way], zz).wait_send()
            y_meta(way, y, zz).wait_send()
            for h in (0, 1):
                y_half(way, y, zz, h).wait_send()
        far_meta(came_up, zz).wait_send()
        for side in (0, 1):
            src = z + zz if side else z - zz

            @pl.when((src >= 0) & (src < NZ) & sides[side][1])
            def _():
                z_meta(side, zz, src).wait_send()
                for h in (0, 1):
                    z_half(side, zz, src, h).wait_send()

        for h in (0, 1):
            @pl.when(zz > z)
            def _():
                z_copy(0, h, zz).wait_send()

            @pl.when(zz < z)
            def _():
                z_copy(1, h, zz).wait_send()

        return carry

    lax.fori_loop(0, NZ, finish, 0)
    for g in range(len(GROUPS)):
        for d in (0, 1):
            for s in range(NR - 1):
                rs_copy(g, d, s).wait_send()
                ag_copy(g, d, s).wait_send()
    for g in (1, 2, 3):
        back_copy(g).wait_send()

    @pl.when(sec > 0)
    def _():
        shift().wait_send()

    @pl.when(sec < NS - 1)
    def _():
        shift().wait_recv()


def layer(tokens, meta, wg, wu, wd):
    dma = pltpu.SemaphoreType.DMA
    vm = pltpu.VMEM
    bf, f32 = jnp.bfloat16, jnp.float32
    rows = NR * ROWS
    return pl.pallas_call(
        kernel,
        out_shape=(jax.ShapeDtypeStruct((TOK, D), bf),) + (jax.ShapeDtypeStruct((D, H), bf),) * 3,
        in_specs=[pl.BlockSpec(memory_space=pltpu.VMEM)] * 5,
        out_specs=(pl.BlockSpec(memory_space=pltpu.VMEM),) * 4,
        scratch_shapes=[
            vm((NY * TOKS, 2 * D), bf), vm((NY * NZ, 16, 128), f32),
            vm((rows, TOKS), bf), vm((NY, ROWS, TOKS), bf),
            vm((rows, D), bf), vm((rows, D), bf), vm((rows, 3 * H), f32),
            vm((NY, 2, 3, PIECE, 384), bf), vm((NY, 2, 3, PIECE, 384), bf),
            vm((2, 3, REST, 384), bf), vm((2, 3, REST, 384), bf),
            vm((2, rows, 384), bf), vm((2, D, 256), bf), vm((2, D, 384), f32),
            vm((NY, ROWS, D), bf), vm((NY, ROWS, D), bf), vm((TOKS, D), f32),
            vm((2, 2, NZ, HALF, D), bf), vm((2, 2, NZ, HALF, D), bf),
            vm((TOK, D), bf), dma((2,)),
        ] + ([dma((2, NZ, 2))] * 2 + [dma((2, NZ))] * 2) * 2 + [dma((2, NZ))] * 2 + [dma((NZ,))] * 2
        + [dma((len(GROUPS), 2, 3))] * 4 + [dma((NY,))] * 2 + [dma((2, 2, NZ))] * 2 + [dma(()), dma(())],
        compiler_params=pltpu.CompilerParams(
            collective_id=0, has_side_effects=True, vmem_limit_bytes=VMEM_LIMIT
        ),
    )(tokens, meta, wg, wu, wd)


def table_of(routes, weights):
    chosen = routes.T[None] == jnp.arange(EXPERTS, dtype=jnp.int32)[:, None, None]
    named = jnp.sum(chosen.astype(jnp.float32), axis=1)
    weight = jnp.sum(jnp.where(chosen, weights.T[None], 0.0), axis=1)
    earlier = (jnp.arange(TOK)[:, None] < jnp.arange(TOK)[None, :]).astype(jnp.bfloat16)
    slot = jnp.dot(named.astype(jnp.bfloat16), earlier, preferred_element_type=jnp.float32)
    slot = jnp.where(named > 0.0, slot, -1.0)
    both = jnp.concatenate([slot, weight], axis=0)
    return jnp.concatenate([both, both], axis=1)


def per_device(token_grads, routing, gate_weights, layer_inputs, w_gate, w_up, w_down):
    block = jnp.concatenate([layer_inputs[0], token_grads[0]], axis=1)
    meta = table_of(routing[0], gate_weights[0])
    upstream, grad_gate, grad_up, grad_down = layer(block, meta, w_gate[0], w_up[0], w_down[0])
    return (upstream[None], grad_gate[None], grad_up[None], grad_down[None])


def solution(mesh):
    placed = (
        P("section", "expert", "replica"),
        P("section", "expert", None),
        P("section", "expert", None),
        P("section", "expert", "replica"),
        P("section", "replica", "expert"),
        P("section", "replica", "expert"),
        P("section", "replica", "expert"),
    )
    return jax.shard_map(
        per_device,
        mesh=mesh,
        in_specs=placed,
        out_specs=(
            P("section", "expert", "replica"),
            P("section", "replica", "expert"),
            P("section", "replica", "expert"),
            P("section", "replica", "expert"),
        ),
        check_vma=False,
    )
```

```python
import jax
import jax.numpy as jnp
from jax import lax
from jax.experimental import pallas as pl
from jax.experimental.pallas import tpu as pltpu
from jax.sharding import PartitionSpec as P

MESH = pl.DeviceIdType.MESH
SHARES = 4
NY, NZ, NR = 4, 8, 4
EXPERTS = 8
TOK = 64
CAP = 34
D = 896
H = 256
ROWS = NZ * CAP
TOKS = NZ * TOK
HALF = TOK // 2
PIECE, REST = 64, 16
COLUMN = (0, 1, 3, 2)
GROUPS = ((0, 0, 32), (1, 0, 64), (2, 0, 64), (3, 0, 64), None, (0, 32, 32))
NS = 8
VMEM_LIMIT = 60 * 1024 * 1024


def remote(src, dst, send_sem, recv_sem, **where):
    return pltpu.make_async_remote_copy(
        src_ref=src, dst_ref=dst, send_sem=send_sem, recv_sem=recv_sem,
        device_id=where, device_id_type=MESH,
    )


def rows_of(ref, start, size):
    return ref.at[pl.ds(pl.multiple_of(start, 16), size), :]


def grid_place():
    me = lax.axis_index("expert")
    y, z = me // NZ, me % NZ
    return me, y, z, (y + 1) % NY * NZ + z, (y + NY - 1) % NY * NZ + z


def over_rows(left, right):
    return lax.dot_general(
        left, right, (((0,), (0,)), ((), ())), preferred_element_type=jnp.float32
    )


def over_cols(left, right):
    return lax.dot_general(
        left, right, (((1,), (1,)), ((), ())), preferred_element_type=jnp.float32
    )


def kernel(b_ref, m_ref, wg, wu, wd, o_ref, gg, gu, gd,
           ball, mall, pick, picks, xs, gs, part, snd, rcv, snd_rest, rcv_rest, act, wcat, gacc,
           bsnd, brcv, total, zsnd, zrcv, edge, own_sem,
           zb_send, zb_recv, zm_send, zm_recv, yb_send, yb_recv, ym_send, ym_recv,
           fb_send, fb_recv, fm_send, fm_recv, rs_send, rs_recv, ag_send, ag_recv,
           b_send, b_recv, z_send, z_recv, s_send, s_recv):
    me, y, z, up, down = grid_place()
    r = lax.axis_index("replica")
    sec = lax.axis_index("section")
    peers = (up, down)
    rings = ((r + 1) % NR, (r + NR - 1) % NR)
    far_off = (y + 2) % NY * NZ + z
    sides = ((me + 1, z < NZ - 1, z > 0), (me - 1, z > 0, z < NZ - 1))

    barrier = pltpu.get_barrier_semaphore()
    for peer in (up, down, far_off):
        pl.semaphore_signal(barrier, inc=1, device_id={"expert": peer}, device_id_type=MESH)
    for peer in rings:
        pl.semaphore_signal(barrier, inc=1, device_id={"replica": peer}, device_id_type=MESH)
    for side in (0, 1):
        @pl.when(sides[side][1])
        def _():
            pl.semaphore_signal(barrier, inc=1, device_id={"expert": sides[side][0]}, device_id_type=MESH)

    for near, there in ((sec - 1, sec > 0), (sec + 1, sec < NS - 1)):
        @pl.when(there)
        def _():
            pl.semaphore_signal(barrier, inc=1, device_id={"section": near}, device_id_type=MESH)

    pl.semaphore_wait(
        barrier, 9 - (NZ - z) // NZ - (z + 1) // NZ - (NS - sec) // NS - (sec + 1) // NS
    )

    own_b = pltpu.make_async_copy(b_ref, rows_of(ball, me * TOK, TOK), own_sem.at[0])
    own_m = pltpu.make_async_copy(m_ref, mall.at[me], own_sem.at[1])
    own_b.start()
    own_m.start()
    own_b.wait()
    own_m.wait()

    def half(at, h):
        return rows_of(ball, at * TOK + h * HALF, HALF)

    def z_half(side, t, zz, h):
        b = half(y * NZ + zz, h)
        return remote(b, b, zb_send.at[side, t, h], zb_recv.at[side, t, h], expert=sides[side][0])

    def z_meta(side, t, zz):
        m = mall.at[y * NZ + zz]
        return remote(m, m, zm_send.at[side, t], zm_recv.at[side, t], expert=sides[side][0])

    def y_half(way, col, zz, h):
        b = half(col * NZ + zz, h)
        return remote(b, b, yb_send.at[way, zz, h], yb_recv.at[way, zz, h], expert=peers[way])

    def y_meta(way, col, zz):
        m = mall.at[col * NZ + zz]
        return remote(m, m, ym_send.at[way, zz], ym_recv.at[way, zz], expert=peers[way])

    def far_copy(way, col, zz):
        b = rows_of(ball, (col * NZ + zz) * TOK + way * HALF, HALF)
        return remote(b, b, fb_send.at[way, zz], fb_recv.at[way, zz], expert=peers[way])

    def far_meta(col, zz):
        at = col * NZ + zz
        return remote(mall.at[at], mall.at[at], fm_send.at[zz], fm_recv.at[zz], expert=up)

    came_up, came_down, far = (y + NY - 1) % NY, (y + 1) % NY, (y + 2) % NY

    def along(t, carry):
        for h in (0, 1):
            for side in (0, 1):
                zz = z + t if side else z - t
                inside = (zz >= 0) & (zz < NZ)

                @pl.when(inside & (t > 0))
                def _():
                    if h == 0:
                        z_meta(side, t - 1, zz).wait_recv()
                    z_half(side, t - 1, zz, h).wait_recv()

                @pl.when(inside & sides[side][1])
                def _():
                    if h == 0:
                        z_meta(side, t, zz).start()
                    z_half(side, t, zz, h).start()

                @pl.when(inside & ((t > 0) if side else (t >= 0)))
                def _():
                    for way in (0, 1):
                        if h == 0:
                            y_meta(way, y, zz).start()
                        y_half(way, y, zz, h).start()

        return carry

    lax.fori_loop(0, NZ, along, 0)

    def round_y(t, carry):
        for side in (0, 1):
            zz = z + t if side else z - t

            @pl.when((zz >= 0) & (zz < NZ) & ((t > 0) if side else (t >= 0)))
            def _():
                y_meta(0, came_up, zz).wait_recv()
                far_meta(came_up, zz).start()
                y_half(0, came_up, zz, 0).wait_recv()
                far_copy(0, came_up, zz).start()
                y_half(1, came_down, zz, 1).wait_recv()
                far_copy(1, came_down, zz).start()

        return carry

    def round_rest(zz, carry):
        y_half(0, came_up, zz, 1).wait_recv()
        y_meta(1, came_down, zz).wait_recv()
        y_half(1, came_down, zz, 0).wait_recv()
        return carry

    def round_far(zz, carry):
        for way in (0, 1):
            far_copy(way, far, zz).wait_recv()
        far_meta(far, zz).wait_recv()
        return carry

    lane = lax.broadcasted_iota(jnp.int32, (1, 128), 1)
    first = lane < TOK
    row = lax.broadcasted_iota(jnp.int32, (ROWS, 128), 0).astype(jnp.float32)
    which = lax.broadcasted_iota(jnp.int32, (NZ, EXPERTS, 128), 1)

    def choose(to, at, c, e):
        meta = mall[pl.ds(c * NZ, NZ)]
        slots = jnp.sum(jnp.where(which == e, meta[:, 0:8, :], 0.0), axis=1)
        scale = jnp.sum(jnp.where(which == e, meta[:, 8:16, :], 0.0), axis=1)
        weight = jnp.zeros((ROWS, 128), jnp.float32)
        for p in range(NZ // 2):
            slot = jnp.where(first, slots[2 * p:2 * p + 1], slots[2 * p + 1:2 * p + 2])
            w = jnp.where(first, scale[2 * p:2 * p + 1], scale[2 * p + 1:2 * p + 2])
            base = jnp.where(first, float(CAP * 2 * p), float(CAP * (2 * p + 1)))
            hit = row == jnp.where(slot >= 0.0, slot + base, -1.0)
            weight = weight + jnp.where(hit, w, 0.0)
            to[pl.ds(pl.multiple_of(at, 16), ROWS), 128 * p:128 * p + 128] = jnp.where(hit, 1.0, 0.0).astype(jnp.bfloat16)
        return jnp.sum(weight, axis=1, keepdims=True)

    def column(g):
        return (y + COLUMN[g]) % NY

    def column_rows(g):
        return pl.ds(pl.multiple_of(column(g) * ROWS, 16), ROWS)

    def products(g):
        c = column(g)
        rows = column_rows(g)
        toks = pl.ds(pl.multiple_of(c * TOKS, 16), TOKS)
        weight = choose(pick, c * ROWS, c, me // SHARES)
        sel = pick[rows, :]
        x = jnp.dot(sel, ball[toks, 0:D], preferred_element_type=jnp.float32).astype(jnp.bfloat16)
        xs[rows, :] = x
        gr = jnp.dot(sel, ball[toks, D:2 * D], preferred_element_type=jnp.float32)
        gr = (gr * weight).astype(jnp.bfloat16)
        gs[rows, :] = gr
        part[rows, 0:256] = jnp.dot(x, wg[...], preferred_element_type=jnp.float32)
        part[rows, 256:512] = jnp.dot(x, wu[...], preferred_element_type=jnp.float32)
        part[rows, 512:768] = jnp.dot(gr, wd[...], preferred_element_type=jnp.float32)

    def piece(g, o):
        if g == NY:
            return pl.ds(pl.multiple_of(o * ROWS + NR * PIECE, 16), REST)
        c, at, size = GROUPS[g]
        return pl.ds(pl.multiple_of(column(c) * ROWS + o * PIECE + at, 16), size)

    def out_of(g, d, s):
        if g == NY:
            return snd_rest.at[d, s], rcv_rest.at[d, s]
        c, at, size = GROUPS[g]
        return snd.at[c, d, s, at:at + size], rcv.at[c, d, s, at:at + size]

    def rs_copy(g, d, s):
        a, b = out_of(g, d, s)
        return remote(a, b, rs_send.at[g, d, s], rs_recv.at[g, d, s], replica=rings[d])

    def stage(g, s):
        for d in (0, 1):
            o = (r + NR - 1 - s) % NR if d == 0 else (r + 1 + s) % NR
            rows = piece(g, o)
            a = out_of(g, d, s)[0]
            if s:
                b = out_of(g, d, s - 1)[1]
                rs_copy(g, d, s - 1).wait_recv()
            for kind in range(3):
                mine = part[rows, 256 * kind + 128 * d:256 * kind + 128 * d + 128]
                cols = slice(128 * kind, 128 * kind + 128)
                if s:
                    mine = mine + b[:, cols].astype(jnp.float32)
                a[:, cols] = mine.astype(jnp.bfloat16)
            rs_copy(g, d, s).start()

    def ag_copy(g, d, s):
        there = act.at[d, piece(g, (r + NR - s) % NR if d == 0 else (r + s) % NR), :]
        return remote(there, there, ag_send.at[g, d, s], ag_recv.at[g, d, s], replica=rings[d])

    def arrived(g, d, s):
        there = act.at[d, piece(g, (r + NR - 1 - s) % NR if d == 0 else (r + 1 + s) % NR), :]
        return remote(there, there, ag_send.at[g, d, s], ag_recv.at[g, d, s], replica=rings[d])

    def final(g):
        for d in (0, 1):
            rs_copy(g, d, 2).wait_recv()
            rows = piece(g, r)
            b = out_of(g, d, 2)[1]
            gate, upp, dh = [
                part[rows, 256 * kind + 128 * d:256 * kind + 128 * d + 128]
                + b[:, 128 * kind:128 * kind + 128].astype(jnp.float32)
                for kind in range(3)
            ]
            sg = jax.nn.sigmoid(gate)
            a = gate * sg
            act[d, rows, 0:128] = (a * upp).astype(jnp.bfloat16)
            act[d, rows, 128:256] = (dh * upp * (sg * (1.0 + gate * (1.0 - sg)))).astype(jnp.bfloat16)
            act[d, rows, 256:384] = (dh * a).astype(jnp.bfloat16)
            ag_copy(g, d, 0).start()

    def onward(g, s):
        for d in (0, 1):
            arrived(g, d, s - 1).wait_recv()
            if s < NR - 1:
                ag_copy(g, d, s).start()

    def back_copy(g):
        to = (me, up, down, far_off)[g]
        return remote(bsnd.at[g], brcv.at[g], b_send.at[g], b_recv.at[g], expert=to)

    def backward(g):
        rows = column_rows(g)
        back = over_cols(act[0, rows, 128:384], wcat[0]) + over_cols(act[1, rows, 128:384], wcat[1])
        if g:
            bsnd[g] = back.astype(jnp.bfloat16)
            back_copy(g).start()
        else:
            brcv[0] = back.astype(jnp.bfloat16)

    def weights(g, fresh):
        rows = column_rows(g)
        both = jnp.concatenate([act[0, rows, 128:384], act[1, rows, 128:384]], axis=1)
        up_down = over_rows(xs[rows, :], both)
        hid = over_rows(gs[rows, :], jnp.concatenate([act[0, rows, 0:128], act[1, rows, 0:128]], axis=1))
        if fresh:
            gacc[:, 0:512] = up_down
            gacc[:, 512:768] = hid
        else:
            gacc[:, 0:512] = gacc[:, 0:512] + up_down
            gacc[:, 512:768] = gacc[:, 512:768] + hid

    def collect(g, fresh):
        if g:
            back_copy(g).wait_recv()
        mine = over_rows(picks[g], brcv[g])
        total[...] = mine if fresh else total[...] + mine

    products(0)
    stage(0, 0)
    stage(5, 0)
    lax.fori_loop(0, NZ, round_y, 0)
    lax.fori_loop(0, NZ, round_rest, 0)
    stage(0, 1)
    stage(5, 1)
    products(1)
    stage(1, 0)
    products(2)
    stage(2, 0)
    stage(0, 2)
    stage(5, 2)
    lax.fori_loop(0, NZ, round_far, 0)
    products(3)
    stage(4, 0)
    stage(3, 0)
    for g in (1, 2, 4, 3):
        stage(g, 1)
    for d in (0, 1):
        wcat[d, :, 0:128] = wg[:, 128 * d:128 * d + 128]
        wcat[d, :, 128:256] = wu[:, 128 * d:128 * d + 128]
    for g in range(NY):
        choose(picks.at[g], 0, y, (y + (0, 3, 1, 2)[g]) % NY * 2 + z // SHARES)
    for g in (1, 2, 4, 3):
        stage(g, 2)
    final(1)
    final(2)
    final(4)
    final(0)
    final(5)
    onward(1, 1)
    final(3)
    onward(4, 1)
    onward(2, 1)
    onward(1, 2)
    onward(3, 1)
    onward(0, 1)
    onward(5, 1)
    onward(4, 2)
    onward(1, 3)
    onward(3, 2)
    onward(2, 2)
    onward(4, 3)
    backward(1)
    onward(3, 3)
    backward(3)
    onward(0, 2)
    onward(5, 2)
    onward(2, 3)
    backward(2)
    weights(1, True)
    weights(3, False)
    collect(1, True)
    collect(3, False)
    collect(2, False)
    onward(0, 3)
    onward(5, 3)
    backward(0)
    collect(0, False)

    def z_copy(side, h, zz):
        return remote(zsnd.at[side, h, zz], zrcv.at[side, h, zz],
                      z_send.at[side, h, zz], z_recv.at[side, h, zz], expert=sides[side][0])

    def of_group(h, zz):
        return total[pl.ds(pl.multiple_of(zz * TOK + h * HALF, 16), HALF), :]

    def slot(tau, carry):
        for h in (0, 1):
            for side in (0, 1):
                zz = tau - (NZ - 1) + z if side else NZ - 1 - tau + z
                live = (zz >= 0) if side else (zz < NZ)

                @pl.when(live & sides[side][1] & sides[side][2])
                def _():
                    z_copy(side, h, zz).wait_recv()
                    zsnd[side, h, zz] = (of_group(h, zz) + zrcv[side, h, zz].astype(jnp.float32)).astype(jnp.bfloat16)
                    z_copy(side, h, zz).start()

                @pl.when(live & sides[side][1] & jnp.logical_not(sides[side][2]))
                def _():
                    zsnd[side, h, zz] = of_group(h, zz).astype(jnp.bfloat16)
                    z_copy(side, h, zz).start()

        return carry

    lax.fori_loop(0, 1, slot, 0)
    weights(2, False)
    weights(0, False)
    lax.fori_loop(1, NZ - 1, slot, 0)
    for h in (0, 1):
        at = pl.ds(pl.multiple_of(z * TOK + h * HALF, 16), HALF)
        for side in (0, 1):
            @pl.when(sides[side][2])
            def _():
                z_copy(side, h, z).wait_recv()
                total[at, :] = total[at, :] + zrcv[side, h, z].astype(jnp.float32)

        edge[h * HALF:h * HALF + HALF, :] = total[at, :].astype(jnp.bfloat16)

    def shift():
        return remote(edge, o_ref, s_send, s_recv, section=sec - 1)

    @pl.when(sec > 0)
    def _():
        shift().start()

    @pl.when(sec == NS - 1)
    def _():
        o_ref[...] = jnp.zeros_like(o_ref)

    for d in (0, 1):
        cols = slice(128 * d, 128 * d + 128)
        gg[:, cols] = gacc[:, 256 * d:256 * d + 128].astype(jnp.bfloat16)
        gu[:, cols] = gacc[:, 256 * d + 128:256 * d + 256].astype(jnp.bfloat16)
        gd[:, cols] = gacc[:, 512 + 128 * d:640 + 128 * d].astype(jnp.bfloat16)

    def finish(zz, carry):
        for way in (0, 1):
            far_copy(way, (came_up, came_down)[way], zz).wait_send()
            y_meta(way, y, zz).wait_send()
            for h in (0, 1):
                y_half(way, y, zz, h).wait_send()
        far_meta(came_up, zz).wait_send()
        for side in (0, 1):
            src = z + zz if side else z - zz

            @pl.when((src >= 0) & (src < NZ) & sides[side][1])
            def _():
                z_meta(side, zz, src).wait_send()
                for h in (0, 1):
                    z_half(side, zz, src, h).wait_send()

        for h in (0, 1):
            @pl.when(zz > z)
            def _():
                z_copy(0, h, zz).wait_send()

            @pl.when(zz < z)
            def _():
                z_copy(1, h, zz).wait_send()

        return carry

    lax.fori_loop(0, NZ, finish, 0)
    for g in range(len(GROUPS)):
        for d in (0, 1):
            for s in range(NR - 1):
                rs_copy(g, d, s).wait_send()
                ag_copy(g, d, s).wait_send()
    for g in (1, 2, 3):
        back_copy(g).wait_send()

    @pl.when(sec > 0)
    def _():
        shift().wait_send()

    @pl.when(sec < NS - 1)
    def _():
        shift().wait_recv()


def layer(tokens, meta, wg, wu, wd):
    dma = pltpu.SemaphoreType.DMA
    vm = pltpu.VMEM
    bf, f32 = jnp.bfloat16, jnp.float32
    rows = NR * ROWS
    return pl.pallas_call(
        kernel,
        out_shape=(jax.ShapeDtypeStruct((TOK, D), bf),) + (jax.ShapeDtypeStruct((D, H), bf),) * 3,
        in_specs=[pl.BlockSpec(memory_space=pltpu.VMEM)] * 5,
        out_specs=(pl.BlockSpec(memory_space=pltpu.VMEM),) * 4,
        scratch_shapes=[
            vm((NY * TOKS, 2 * D), bf), vm((NY * NZ, 16, 128), f32),
            vm((rows, TOKS), bf), vm((NY, ROWS, TOKS), bf),
            vm((rows, D), bf), vm((rows, D), bf), vm((rows, 3 * H), f32),
            vm((NY, 2, 3, PIECE, 384), bf), vm((NY, 2, 3, PIECE, 384), bf),
            vm((2, 3, REST, 384), bf), vm((2, 3, REST, 384), bf),
            vm((2, rows, 384), bf), vm((2, D, 256), bf), vm((D, 768), f32),
            vm((NY, ROWS, D), bf), vm((NY, ROWS, D), bf), vm((TOKS, D), f32),
            vm((2, 2, NZ, HALF, D), bf), vm((2, 2, NZ, HALF, D), bf),
            vm((TOK, D), bf), dma((2,)),
        ] + ([dma((2, NZ, 2))] * 2 + [dma((2, NZ))] * 2) * 2 + [dma((2, NZ))] * 2 + [dma((NZ,))] * 2
        + [dma((len(GROUPS), 2, 3))] * 4 + [dma((NY,))] * 2 + [dma((2, 2, NZ))] * 2 + [dma(()), dma(())],
        compiler_params=pltpu.CompilerParams(
            collective_id=0, has_side_effects=True, vmem_limit_bytes=VMEM_LIMIT
        ),
    )(tokens, meta, wg, wu, wd)


def table_of(routes, weights):
    chosen = routes.T[None] == jnp.arange(EXPERTS, dtype=jnp.int32)[:, None, None]
    named = jnp.sum(chosen.astype(jnp.float32), axis=1)
    weight = jnp.sum(jnp.where(chosen, weights.T[None], 0.0), axis=1)
    earlier = (jnp.arange(TOK)[:, None] < jnp.arange(TOK)[None, :]).astype(jnp.bfloat16)
    slot = jnp.dot(named.astype(jnp.bfloat16), earlier, preferred_element_type=jnp.float32)
    slot = jnp.where(named > 0.0, slot, -1.0)
    both = jnp.concatenate([slot, weight], axis=0)
    return jnp.concatenate([both, both], axis=1)


def per_device(token_grads, routing, gate_weights, layer_inputs, w_gate, w_up, w_down):
    block = jnp.concatenate([layer_inputs[0], token_grads[0]], axis=1)
    meta = table_of(routing[0], gate_weights[0])
    upstream, grad_gate, grad_up, grad_down = layer(block, meta, w_gate[0], w_up[0], w_down[0])
    return (upstream[None], grad_gate[None], grad_up[None], grad_down[None])


def solution(mesh):
    placed = (
        P("section", "expert", "replica"),
        P("section", "expert", None),
        P("section", "expert", None),
        P("section", "expert", "replica"),
        P("section", "replica", "expert"),
        P("section", "replica", "expert"),
        P("section", "replica", "expert"),
    )
    return jax.shard_map(
        per_device,
        mesh=mesh,
        in_specs=placed,
        out_specs=(
            P("section", "expert", "replica"),
            P("section", "replica", "expert"),
            P("section", "replica", "expert"),
            P("section", "replica", "expert"),
        ),
        check_vma=False,
    )
```
